32 devices in a mesh: req: 4 (over z), seq: 8 (over y, x, core).
Axes of the slice: x: 2, y: 2, z: 4, core: 2. Of those that a mesh axis runs over, the one named last changes fastest.
Arguments:
- hidden_in: bfloat16 [4, 32, 4, 2048], P(None, 'req', None, 'seq'), may hold values from -30 to 30
- cache_lens: int32 [32], P('req'), may hold values from 1 to 4092, as said below
- page_table: int32 [32, 32], P('req'), may hold values from -1 to 55, as said below
- key_cache: bfloat16 [224, 128, 1024], P(('req', 'seq')), may hold values from -250 to 250
- value_cache: bfloat16 [224, 128, 1024], P(('req', 'seq')), may hold values from -4 to 4
- norm_attn: float32 [8192], replicated, may hold values from 0.1 to 1.9
- w_qkv: bfloat16 [8192, 10240], P(None, 'seq'), may hold values from -0.0625 to 0.0625
- b_qkv: bfloat16 [10240], P('seq'), may hold values from -3 to 3
- w_out: bfloat16 [8192, 4, 2048], P(None, None, 'seq'), may hold values from -0.25 to 0.25
- norm_mlp: float32 [8192], replicated, may hold values from 0.1 to 1.9
- w_gate: bfloat16 [8192, 29568], P('req', 'seq'), may hold values from -0.0625 to 0.0625
- w_up: bfloat16 [8192, 29568], P('req', 'seq'), may hold values from -0.0625 to 0.0625
- w_down: bfloat16 [29568, 8192], P('seq', 'req'), may hold values from -0.03125 to 0.03125
Outputs:
- hidden_out: bfloat16 [4, 32, 4, 2048], P(None, 'req', None, 'seq')
- key_cache_out: bfloat16 [224, 128, 1024], P(('req', 'seq'))
- value_cache_out: bfloat16 [224, 128, 1024], P(('req', 'seq'))
The draws below stay inside these ranges and needn't reach their ends.
Inputs may be any that keep to these rules, and one draw needn't show every extreme that they name: `cache_lens`: in each group of 8 requests exactly one holds 4092 tokens and one holds 380; every other one holds at most 380. For request r and logical page j below ceil((cache_lens[r]+4)/128), page_table[r, j] is a slot of the group's 56 page slots (slot s*7+p is the p-th slot of seq index s); no slot is named twice within a group; all other entries are -1.
All inputs are finite; a program needn't handle non-finite values.
Results may differ from the reference program's by a relative error of at most 0.012.
The reference program's roundings to bfloat16 on the way count: a program that leaves them out, or rounds other values in their place, can miss the bound.
Values may be sent and summed in bfloat16 or wider, within the bound.
A program may use at most 320 MiB of HBM per device.

```python
import math
import jax
import jax.numpy as jnp
from jax import lax

D = 8192
H = 64
KV = 8
HD = 128
FF = 29568
STEPS = 4
PAGE = 128
PMAX = 32
RG = 8
GROUPS = 4
R = 32
WIDTH_PART = 2048
QKVW = 10240
POOL = 56
NPAGES = 224
LONGEST = 4096
SHORT_PAGES = 3


def plan_group(key):
    keys = jax.random.split(key, 4)
    short_top = SHORT_PAGES * PAGE - STEPS
    first = jax.random.randint(keys[0], (RG,), 0, short_top)
    second = jax.random.randint(keys[1], (RG,), 0, short_top)
    lengths = 1 + first * second // short_top
    longest = jax.random.randint(keys[2], (), 0, RG)
    index = jnp.arange(RG)
    lengths = jnp.where(index == longest, LONGEST - STEPS, jnp.where(index == (longest + 1) % RG, short_top, lengths))
    pages = (lengths + STEPS + PAGE - 1) // PAGE
    order = jax.random.permutation(keys[3], POOL)
    order = jnp.where(order == POOL - 1, order[0], order).at[0].set(POOL - 1)
    starts = jnp.cumsum(pages) - pages
    column = jnp.arange(PMAX)
    entry = order[jnp.clip(starts[:, None] + column[None, :], 0, POOL - 1)]
    table = jnp.where(column[None, :] < pages[:, None], entry, -1)
    return (lengths.astype(jnp.int32), table.astype(jnp.int32))


def plan_all(key):
    keys = jax.random.split(jax.random.fold_in(key, 11), R // RG)
    return jax.vmap(plan_group)(keys)


def draw_cache_lens(key, part):
    lengths, table = plan_all(key)
    return lengths.reshape(R)


def draw_page_table(key, part):
    lengths, table = plan_all(key)
    return table.reshape(R, PMAX)


def draw_hidden_in(key, part):
    groups = R // RG
    width = D // groups
    keys = jax.random.split(key, 3)
    shape = (STEPS, R, groups, width)
    column = jnp.arange(D, dtype=jnp.float32).reshape(1, 1, groups, width) / D
    factor = jnp.exp(jax.random.uniform(keys[1], (1, 1, groups, width), minval=0.0, maxval=math.log(3.5)))
    rows = jnp.exp(jax.random.uniform(keys[2], (STEPS, R, 1, 1), minval=math.log(0.6), maxval=math.log(1.7)))
    noise = jnp.clip(jax.random.normal(keys[0], shape), -4.0, 4.0)
    ramp = 0.25 * 3.0 ** column
    return (noise * ramp * factor * rows).astype(jnp.bfloat16)


def draw_key_cache(key, part):
    shape = (NPAGES, PAGE // 2, 2, KV * HD)
    keys = jax.random.split(key, 1)
    base = jnp.clip(jax.random.normal(keys[0], shape), -4.0, 4.0)
    return base.reshape(NPAGES, PAGE, KV * HD).astype(jnp.bfloat16)


def block_levels(stream_key, dims, shards, low, top_value):
    level = 1.0
    for axis_at, blocks in shards:
        draws = jax.random.uniform(jax.random.fold_in(jax.random.fold_in(stream_key, 6), axis_at), (blocks,), jnp.float32, low / len(shards), top_value / len(shards))
        level = level * jnp.repeat(jnp.exp(draws), dims[axis_at] // blocks).reshape((-1,) + (1,) * (len(dims) - 1 - axis_at))
    return level


def scatter_about(stream_key, shape, spread, most, cuts=(), kind=jnp.bfloat16):
    values = jax.random.normal(stream_key, shape, jnp.float32) * spread
    if len(cuts) > 0:
        values = block_levels(stream_key, shape, cuts, -0.22, 0.18) * values
    return jnp.clip(values, min=-most, max=most).astype(kind)


def setup_inputs(seed: int = 0) -> dict:
    key_list = jax.random.split(jax.random.key(seed), 14)
    return {
        "hidden_in": draw_hidden_in(jax.random.fold_in(key_list[13], 71), 0),
        "cache_lens": draw_cache_lens(jax.random.fold_in(key_list[13], 71), 0),
        "page_table": draw_page_table(jax.random.fold_in(key_list[13], 71), 0),
        "key_cache": draw_key_cache(jax.random.fold_in(key_list[13], 71), 0),
        "value_cache": scatter_about(key_list[4], (NPAGES, PAGE, KV * HD), 1.0, 4.0, ((0, 32),)),
        "norm_attn": jnp.clip(1.0 + 0.18 * jax.random.normal(key_list[5], (D,), jnp.float32), 0.1, 1.9),
        "w_qkv": scatter_about(key_list[6], (D, QKVW), D ** -0.5, 0.0625, ((1, 8),)),
        "b_qkv": scatter_about(key_list[7], (QKVW,), 0.5, 3.0, ((0, 8),)),
        "w_out": scatter_about(key_list[8], (H * HD, GROUPS, WIDTH_PART), (H * HD // 16) ** -0.5, 0.25, ((2, 8),)),
        "norm_mlp": jnp.clip(1.0 + 0.18 * jax.random.normal(key_list[9], (D,), jnp.float32), 0.1, 1.9),
        "w_gate": scatter_about(key_list[10], (D, FF), D ** -0.5, 0.0625, ((0, 4), (1, 8))),
        "w_up": scatter_about(key_list[11], (D, FF), D ** -0.5, 0.0625, ((0, 4), (1, 8))),
        "w_down": scatter_about(key_list[12], (FF, D), FF ** -0.5, 0.03125, ((0, 8), (1, 4))),
    }


EPSILON = 1e-06
THETA = 1000000.0
NEGATIVE = -1e+30

def rotate(heads, position):
    half = heads.shape[-1] // 2
    freq = THETA ** (-(jnp.arange(half, dtype=jnp.float32) * 2.0 / heads.shape[-1]))
    angle = position.astype(jnp.float32)[:, None, None] * freq[None, None, :]
    cosine = jnp.cos(angle)
    sine = jnp.sin(angle)
    first = heads[..., :half]
    second = heads[..., half:]
    return jnp.concatenate([first * cosine - second * sine, second * cosine + first * sine], axis=-1)

def normalize(values, gain):
    return values * lax.rsqrt(lax.optimization_barrier(jnp.mean(values * values, axis=1, keepdims=True)) + EPSILON) * gain

def reference(hidden_in, cache_lens, page_table, key_cache, value_cache, norm_attn, w_qkv, b_qkv, w_out, norm_mlp, w_gate, w_up, w_down):
    group = H // KV
    scale = 1.0 / math.sqrt(HD)
    blocks = R // RG
    owner_group = jnp.arange(R, dtype=jnp.int32) // RG
    used = page_table >= 0
    global_pages = jnp.where(used, page_table + owner_group[:, None] * POOL, 0).astype(jnp.int32)
    offsets = jnp.arange(PMAX, dtype=jnp.int32)[:, None] * PAGE + jnp.arange(PAGE, dtype=jnp.int32)[None, :]
    w_out_flat = w_out.reshape(H * HD, D)
    outputs = []
    for step in range(STEPS):
        current = hidden_in[step].reshape(R, D).astype(jnp.float32)
        normed = normalize(current, norm_attn).astype(jnp.bfloat16)
        projected = (jnp.dot(normed, w_qkv, preferred_element_type=jnp.float32) + b_qkv.astype(jnp.float32)).astype(jnp.bfloat16)
        position = (cache_lens + step).astype(jnp.int32)
        queries = rotate(projected[:, :H * HD].reshape(R, H, HD).astype(jnp.float32), position).astype(jnp.bfloat16)
        new_keys = rotate(projected[:, H * HD:(H + KV) * HD].reshape(R, KV, HD).astype(jnp.float32), position).astype(jnp.bfloat16).reshape(R, KV * HD)
        new_values = projected[:, (H + KV) * HD:]
        target = jnp.take_along_axis(global_pages, (position // PAGE)[:, None].astype(jnp.int32), axis=1)[:, 0]
        inside = (position % PAGE).astype(jnp.int32)
        key_cache = key_cache.at[target, inside].set(new_keys)
        value_cache = value_cache.at[target, inside].set(new_values)

        def attend(inputs):
            query, pages, live, last = inputs
            keys = key_cache[pages].reshape(PMAX, PAGE, KV, HD).astype(jnp.float32)
            values = value_cache[pages].reshape(PMAX, PAGE, KV, HD).astype(jnp.float32)
            valid = jnp.logical_and(live[:, None], offsets <= last)[:, None, None, :]
            scores = jnp.einsum('kgd,jpkd->jkgp', query.reshape(KV, group, HD).astype(jnp.float32), keys, precision=lax.Precision.HIGHEST) * scale
            masked = jnp.where(valid, scores, NEGATIVE)
            page_max = lax.optimization_barrier(jnp.max(masked, axis=3))
            weights = jnp.where(valid, jnp.exp(masked - page_max[..., None]), 0.0).astype(jnp.bfloat16)
            weights = lax.optimization_barrier(weights).astype(jnp.float32)
            page_sum = lax.optimization_barrier(jnp.sum(weights, axis=3))
            page_acc = jnp.einsum('jkgp,jpkd->jkgd', weights, values, precision=lax.Precision.HIGHEST)
            top = lax.optimization_barrier(jnp.max(page_max, axis=0))
            factor = jnp.exp(page_max - top[None])
            total = lax.optimization_barrier(jnp.sum(factor * page_sum, axis=0))
            summed = lax.optimization_barrier(jnp.sum(factor[..., None] * page_acc, axis=0))
            return (summed / total[..., None]).reshape(H, HD)
        attended = lax.map(attend, (queries, global_pages, used, position)).reshape(R, H * HD).astype(jnp.bfloat16)
        middle = (current + jnp.dot(attended, w_out_flat, preferred_element_type=jnp.float32)).astype(jnp.bfloat16)
        middle_f = middle.astype(jnp.float32)
        normed_mid = normalize(middle_f, norm_mlp).astype(jnp.bfloat16)
        gate = jnp.dot(normed_mid, w_gate, preferred_element_type=jnp.float32)
        upward = jnp.dot(normed_mid, w_up, preferred_element_type=jnp.float32)
        hidden = (jax.nn.silu(gate) * upward).astype(jnp.bfloat16)
        result = (middle_f + jnp.dot(hidden, w_down, preferred_element_type=jnp.float32)).astype(jnp.bfloat16)
        outputs.append(result.reshape(R, blocks, D // blocks))
    return (jnp.stack(outputs), key_cache, value_cache)
```

```python
import functools
import math

import jax
import jax.numpy as jnp
from jax import lax
from jax.experimental import pallas as pl
from jax.experimental.pallas import tpu as pltpu
from jax.sharding import PartitionSpec as P

D = 8192
H = 64
KV = 8
HD = 128
STEPS = 4


EPSILON = 1e-06
THETA = 1000000.0
NEGATIVE = -1e30


def rotate(heads, position):
    half = heads.shape[-1] // 2
    freq = THETA ** (-(jnp.arange(half, dtype=jnp.float32) * 2.0 / heads.shape[-1]))
    angle = position.astype(jnp.float32)[:, None, None] * freq[None, None, :]
    cosine = jnp.cos(angle)
    sine = jnp.sin(angle)
    first = heads[..., :half]
    second = heads[..., half:]
    return jnp.concatenate(
        [first * cosine - second * sine, second * cosine + first * sine], axis=-1
    )


MESH = pl.DeviceIdType.MESH


def greet(partners):
    barrier = pltpu.get_barrier_semaphore()
    for partner in partners:
        pl.semaphore_signal(barrier, inc=1, device_id=partner, device_id_type=MESH)
    pl.semaphore_wait(barrier, len(partners))


def remote(src, dst, send, recv, partner):
    return pltpu.make_async_remote_copy(
        src_ref=src,
        dst_ref=dst,
        send_sem=send,
        recv_sem=recv,
        device_id=partner,
        device_id_type=MESH,
    )


def mlp_kernel(
    zs,
    ss,
    width,
    mid_ref,
    norm_ref,
    wg_hbm,
    wu_hbm,
    wd_hbm,
    out_ref,
    wg,
    wu,
    wd,
    cut,
    square,
    got,
    got_sq,
    normed,
    own_g,
    own_u,
    send_r,
    recv_r,
    send_l,
    recv_l,
    hid,
    down,
    parts,
    landed,
    sums,
    back,
    w_sem,
    a_send,
    a_recv,
    b_send,
    b_recv,
    rs_send,
    rs_recv,
    ag_send,
    ag_recv,
    d_send,
    d_recv,
    e_send,
    e_recv,
):
    z = lax.axis_index("req")
    s = lax.axis_index("seq")
    f32 = jnp.float32
    rows = mid_ref.shape[0]
    pieces = mid_ref.shape[1] // zs
    units = wg.shape[0]
    half = zs * rows // 2
    loads = [
        pltpu.make_async_copy(wg_hbm, wg, w_sem.at[0]),
        pltpu.make_async_copy(wu_hbm, wu, w_sem.at[1]),
        pltpu.make_async_copy(wd_hbm, wd, w_sem.at[2]),
    ]
    for load in loads:
        load.start()
    z_partners = [{"req": lax.rem(z + k, zs), "seq": s} for k in range(1, zs)]
    s_partners = [{"req": z, "seq": lax.rem(s + k, ss)} for k in range(1, ss)]

    total = jnp.zeros((8, rows), f32)
    for block in range(zs):
        piece = mid_ref[:, block * pieces : (block + 1) * pieces]
        cut[block] = piece
        value = piece.astype(f32)
        total += lax.dot_general(
            jnp.ones((8, pieces), f32),
            value * value,
            (((1,), (1,)), ((), ())),
            precision=lax.Precision.HIGHEST,
            preferred_element_type=f32,
        )
    square[...] = jnp.zeros_like(square)
    square[:, :rows] = total
    greet(z_partners + s_partners)
    first = []
    for k in range(1, zs):
        to = lax.rem(z + k, zs)
        first.append(
            remote(cut.at[to], got.at[s, z], a_send.at[0, k], a_recv.at[0, k], z_partners[k - 1])
        )
        first.append(
            remote(square, got_sq.at[s, z], a_send.at[1, k], a_recv.at[1, k], z_partners[k - 1])
        )
    for copy in first:
        copy.start()
    got[s, z] = cut[z]
    got_sq[s, z] = square[...]
    for copy in first:
        copy.wait_recv()
    second = []
    for k in range(1, ss):
        second.append(
            remote(got.at[s], got.at[s], b_send.at[0, k], b_recv.at[0, k], s_partners[k - 1])
        )
        second.append(
            remote(got_sq.at[s], got_sq.at[s], b_send.at[1, k], b_recv.at[1, k], s_partners[k - 1])
        )
    for copy in second:
        copy.start()
    for copy in second:
        copy.wait_recv()
    for group in range(zs):
        line = got_sq[0, group]
        for other in range(1, ss):
            line = line + got_sq[other, group]
        spread = lax.dot_general(
            line[:, :rows],
            jnp.full((8, 128), 0.125, f32),
            (((0,), (0,)), ((), ())),
            precision=lax.Precision.HIGHEST,
            preferred_element_type=f32,
        )
        inverse = lax.rsqrt(spread / D + EPSILON)[:, :1]
        for other in range(ss):
            gain = norm_ref[:, other * pieces : (other + 1) * pieces]
            normed[group * rows : (group + 1) * rows, other * pieces : (other + 1) * pieces] = (
                got[other, group].astype(f32) * inverse * gain
            ).astype(jnp.bfloat16)

    starts = list(range(0, units, width))
    count = len(starts)
    sizes = [min(width, units - start) for start in starts]
    padded = [-(-size // 128) * 128 for size in sizes]
    if sizes[-1] != padded[-1]:
        send_r[count - 1] = jnp.zeros_like(send_r[count - 1])
        send_l[count - 1] = jnp.zeros_like(send_l[count - 1])
        hid[count - 1] = jnp.zeros_like(hid[count - 1])
    down[...] = jnp.zeros_like(down)
    loads[0].wait()
    loads[1].wait()

    right = {"req": lax.rem(z + 1, zs), "seq": s}
    left = {"req": lax.rem(z + zs - 1, zs), "seq": s}

    def reduce_copy(way, p):
        src, dst, to = ((send_r, recv_r, right), (send_l, recv_l, left))[way]
        lanes = pl.ds(0, 2 * padded[p])
        return remote(
            src.at[p, :, lanes], dst.at[p, :, lanes], rs_send.at[way, p], rs_recv.at[way, p], to
        )

    def hidden_copy(way, p):
        place = (p, pl.ds(half * (1 - way), half), pl.ds(0, padded[p]))
        return remote(
            hid.at[place],
            hid.at[place],
            ag_send.at[way, p],
            ag_recv.at[way, p],
            (left, right)[way],
        )

    def reduce_step(way, p, place):
        size, pad = sizes[p], padded[p]
        base = half * (1 - way)
        cols = slice(starts[p], starts[p] + size)
        gate = own_g[base : base + half, cols]
        up = own_u[base : base + half, cols]
        if place > 0:
            reduce_copy(way, p).wait_recv()
            came = (recv_r, recv_l)[way]
            gate = gate + came[p, :, :size].astype(f32)
            up = up + came[p, :, pad : pad + size].astype(f32)
        if place < zs - 1:
            goes = (send_r, send_l)[way]
            goes[p, :, :size] = gate.astype(jnp.bfloat16)
            goes[p, :, pad : pad + size] = up.astype(jnp.bfloat16)
            reduce_copy(way, p).start()
        else:
            gate = gate.astype(jnp.bfloat16).astype(f32)
            up = up.astype(jnp.bfloat16).astype(f32)
            hid[p, base : base + half, :size] = (gate / (1.0 + jnp.exp(-gate)) * up).astype(
                jnp.bfloat16
            )
            hidden_copy(way, p).start()

    def down_step(p):
        down[...] += jnp.dot(
            hid[p, :, : sizes[p]],
            wd[starts[p] : starts[p] + sizes[p], :],
            preferred_element_type=f32,
        )

    nt = (((1,), (1,)), ((), ()))
    lag = [0, 1, 3, 5, 7, 9, 11, 13, 15, 17]
    last = lag[2 * zs - 2]
    for i in range(count + last):
        if i < count:
            cols = slice(starts[i], starts[i] + sizes[i])
            own_g[:, cols] = lax.dot_general(normed[...], wg[cols, :], nt, preferred_element_type=f32)
            own_u[:, cols] = lax.dot_general(normed[...], wu[cols, :], nt, preferred_element_type=f32)
        for zz in range(zs):

            @pl.when(z == zz)
            def _(zz=zz, i=i):
                order = (0, 1) if zz < zs // 2 else (1, 0)
                for way in order:
                    place = zz if way == 0 else zs - 1 - zz
                    p = i - lag[place]
                    if 0 <= p < count:
                        reduce_step(way, p, place)
                for way in order[::-1]:
                    place = zs - 1 - zz if way == 0 else zz
                    p = i - lag[zs - 1 + place]
                    if place > 0 and 0 <= p < count:
                        hidden_copy(way, p).wait_recv()
                        if place < zs - 1:
                            hidden_copy(way, p).start()

        if i == last:
            loads[2].wait()
        if i >= last:
            down_step(i - last)

    for other in range(ss):
        parts[other] = down[:, other * pieces : (other + 1) * pieces].astype(jnp.bfloat16)
    third = []
    for k in range(1, ss):
        to = lax.rem(s + k, ss)
        third.append(
            remote(parts.at[to], landed.at[s], d_send.at[k], d_recv.at[k], s_partners[k - 1])
        )
    for copy in third:
        copy.start()
    landed[s] = parts[s]
    for copy in third:
        copy.wait_recv()
    whole = landed[0].astype(f32)
    for other in range(1, ss):
        whole = whole + landed[other].astype(f32)
    for group in range(zs):
        sums[group] = whole[group * rows : (group + 1) * rows]
    fourth = []
    for k in range(1, zs):
        to = lax.rem(z + k, zs)
        fourth.append(
            remote(sums.at[to], back.at[z], e_send.at[k], e_recv.at[k], z_partners[k - 1])
        )
    for copy in fourth:
        copy.start()
    back[z] = sums[z]
    for copy in fourth:
        copy.wait_recv()
    for block in range(zs):
        cols = slice(block * pieces, (block + 1) * pieces)
        out_ref[:, cols] = (mid_ref[:, cols].astype(f32) + back[block]).astype(jnp.bfloat16)

    for copy in first + second + third + fourth:
        copy.wait_send()
    for way in range(2):
        for p in range(count):

            @pl.when(z != (zs - 1 if way == 0 else 0))
            def _(way=way, p=p):
                reduce_copy(way, p).wait_send()

            @pl.when(z != (0 if way == 0 else zs - 1))
            def _(way=way, p=p):
                hidden_copy(way, p).wait_send()


def mlp(middle, norm, w_gate, w_up, w_down, zs, ss):
    rows, features = middle.shape
    pieces = features // zs
    units, depth = w_gate.shape
    quarter = w_down.shape[1]
    width = 512
    count = -(-units // width)
    everyone = zs * rows
    half = everyone // 2
    bf16, f32 = jnp.bfloat16, jnp.float32
    vmem = pl.BlockSpec(memory_space=pltpu.VMEM)
    hbm = pl.BlockSpec(memory_space=pl.ANY)
    dma = pltpu.SemaphoreType.DMA
    return pl.pallas_call(
        functools.partial(mlp_kernel, zs, ss, width),
        name="mlp",
        out_shape=jax.ShapeDtypeStruct(middle.shape, bf16),
        in_specs=[vmem, vmem, hbm, hbm, hbm],
        out_specs=vmem,
        scratch_shapes=[
            pltpu.VMEM(w_gate.shape, bf16),
            pltpu.VMEM(w_up.shape, bf16),
            pltpu.VMEM(w_down.shape, bf16),
            pltpu.VMEM((zs, rows, pieces), bf16),
            pltpu.VMEM((8, 128), f32),
            pltpu.VMEM((ss, zs, rows, pieces), bf16),
            pltpu.VMEM((ss, zs, 8, 128), f32),
            pltpu.VMEM((everyone, depth), bf16),
            pltpu.VMEM((everyone, units), f32),
            pltpu.VMEM((everyone, units), f32),
            pltpu.VMEM((count, half, 2 * width), bf16),
            pltpu.VMEM((count, half, 2 * width), bf16),
            pltpu.VMEM((count, half, 2 * width), bf16),
            pltpu.VMEM((count, half, 2 * width), bf16),
            pltpu.VMEM((count, everyone, width), bf16),
            pltpu.VMEM((everyone, quarter), f32),
            pltpu.VMEM((ss, everyone, pieces), bf16),
            pltpu.VMEM((ss, everyone, pieces), bf16),
            pltpu.VMEM((zs, rows, pieces), f32),
            pltpu.VMEM((zs, rows, pieces), f32),
            dma((3,)),
            dma((2, zs)),
            dma((2, zs)),
            dma((2, ss)),
            dma((2, ss)),
            dma((2, count)),
            dma((2, count)),
            dma((2, count)),
            dma((2, count)),
            dma((ss,)),
            dma((ss,)),
            dma((zs,)),
            dma((zs,)),
        ],
        compiler_params=pltpu.CompilerParams(
            collective_id=0, has_side_effects=True, vmem_limit_bytes=63 * 2**20
        ),
    )(middle, norm, w_gate, w_up, w_down)


def project_kernel(
    zs,
    ss,
    steps,
    lens_ref,
    x_ref,
    norm_ref,
    bias_ref,
    w_hbm,
    q_ref,
    new_ref,
    w,
    own,
    got,
    normed,
    sent,
    columns,
    spread,
    w_sem,
    a_send,
    a_recv,
    b_send,
    b_recv,
):
    z = lax.axis_index("req")
    s = lax.axis_index("seq")
    f32 = jnp.float32
    rows, features = x_ref.shape
    requests = rows // steps
    blocks = zs
    pieces = features // blocks
    mine = w.shape[1]
    local = mine // HD
    group = H // KV
    parts = 4
    depth = D // parts
    loads = [
        pltpu.make_async_copy(
            w_hbm.at[pl.ds(part * depth, depth)], w.at[pl.ds(part * depth, depth)], w_sem.at[part]
        )
        for part in range(parts)
    ]
    for load in loads:
        load.start()
    partners = [{"req": z, "seq": lax.rem(s + k, ss)} for k in range(1, ss)]
    own[...] = x_ref[...]
    greet(partners)
    first = [
        remote(own, got.at[s], a_send.at[k], a_recv.at[k], partners[k - 1]) for k in range(1, ss)
    ]
    for copy in first:
        copy.start()
    got[s] = own[...]
    row = lax.broadcasted_iota(jnp.int32, (rows, HD), 0)
    position = lax.div(row, requests)
    for request in range(requests):
        position = position + jnp.where(lax.rem(row, requests) == request, lens_ref[request], 0)
    lane = lax.broadcasted_iota(jnp.int32, (rows, HD), 1)
    entry = lax.rem(lane, HD // 2).astype(f32)
    angle = position.astype(f32) * jnp.exp(entry * (-2.0 * math.log(THETA) / HD))
    cosine = jnp.cos(angle)
    sine = jnp.where(lane < HD // 2, -jnp.sin(angle), jnp.sin(angle))
    for copy in first:
        copy.wait_recv()
    total = jnp.zeros((rows, 1), f32)
    for other in range(ss):
        value = got[other].astype(f32)
        total += jnp.sum(value * value, axis=1, keepdims=True)
    inverse = lax.rsqrt(total / D + EPSILON)
    for other in range(ss):
        for block in range(blocks):
            base = block * ss * pieces + other * pieces
            for line in range(pieces // 128):
                at = base + line * 128
                value = got[
                    other, :, block * pieces + line * 128 : block * pieces + (line + 1) * 128
                ].astype(f32)
                gain = norm_ref[at // 128 : at // 128 + 1, :]
                normed[:, at : at + 128] = (value * inverse * gain).astype(jnp.bfloat16)
    result = jnp.zeros((rows, mine), f32)
    for part in range(parts):
        loads[part].wait()
        span = slice(part * depth, (part + 1) * depth)
        result += jnp.dot(normed[:, span], w[span, :], preferred_element_type=f32)
    result = (result + bias_ref[...].astype(f32)).astype(jnp.bfloat16).astype(f32)
    for head in range(local):
        tile = result[:, head * HD : (head + 1) * HD]
        turned = tile * cosine + pltpu.roll(tile, HD // 2, axis=1) * sine
        sent[:, head * HD : (head + 1) * HD] = jnp.where(
            s * local + head < H + KV, turned, tile
        ).astype(jnp.bfloat16)
    second = [
        remote(sent, columns.at[s], b_send.at[k], b_recv.at[k], partners[k - 1])
        for k in range(1, ss)
    ]
    for copy in second:
        copy.start()
    columns[s] = sent[...]
    for copy in second:
        copy.wait_recv()
    for head in range(H + 2 * KV):
        other, at = head // local, (head % local) * HD
        tile = columns[other, :, at : at + HD].astype(f32)
        if head < H:
            for step in range(steps):
                base = (head // group) * steps * group + step * group + head % group
                spread[pl.ds(base, requests, stride=H * steps), :] = tile[
                    step * requests : (step + 1) * requests
                ]
        else:
            at = ((head - H) % KV) * HD
            new_ref[(head - H) // KV, :, at : at + HD] = tile
    q_ref[...] = spread[...].astype(jnp.bfloat16)
    for copy in first + second:
        copy.wait_send()


def project(lens, x, norm, bias, w, zs, ss, steps):
    rows, features = x.shape
    mine = w.shape[1]
    bf16, f32 = jnp.bfloat16, jnp.float32
    vmem = pl.BlockSpec(memory_space=pltpu.VMEM)
    dma = pltpu.SemaphoreType.DMA
    return pl.pallas_call(
        functools.partial(project_kernel, zs, ss, steps),
        name="project",
        out_shape=(
            jax.ShapeDtypeStruct((rows * H, HD), bf16),
            jax.ShapeDtypeStruct((2, rows, KV * HD), f32),
        ),
        in_specs=[
            pl.BlockSpec(memory_space=pltpu.SMEM),
            vmem,
            vmem,
            vmem,
            pl.BlockSpec(memory_space=pl.ANY),
        ],
        out_specs=(vmem, vmem),
        scratch_shapes=[
            pltpu.VMEM(w.shape, bf16),
            pltpu.VMEM((rows, features), bf16),
            pltpu.VMEM((ss, rows, features), bf16),
            pltpu.VMEM((rows, D), bf16),
            pltpu.VMEM((rows, mine), bf16),
            pltpu.VMEM((ss, rows, mine), bf16),
            pltpu.VMEM((rows * H, HD), f32),
            dma((4,)),
            dma((ss,)),
            dma((ss,)),
            dma((ss,)),
            dma((ss,)),
        ],
        compiler_params=pltpu.CompilerParams(
            collective_id=1, has_side_effects=True, vmem_limit_bytes=48 * 2**20
        ),
    )(lens, x, norm, bias, w)


def attend_kernel(
    steps,
    table_ref,
    lens_ref,
    q_ref,
    new_ref,
    k_hbm,
    v_hbm,
    acc_ref,
    stat_ref,
    ko_hbm,
    vo_hbm,
    keys,
    values,
    wide,
    scores,
    probs,
    acc,
    in_sem,
    out_sem,
):
    f32, bf16 = jnp.float32, jnp.bfloat16
    slots, page, _ = keys.shape
    requests, most = table_ref.shape
    group = H // KV
    lines = steps * group
    block = KV * lines
    loads = [
        (
            pltpu.make_async_copy(k_hbm.at[j], keys.at[j], in_sem.at[0, j]),
            pltpu.make_async_copy(v_hbm.at[j], values.at[j], in_sem.at[1, j]),
        )
        for j in range(slots)
    ]
    for load in loads:
        load[0].start()
    for load in loads:
        load[1].start()
    stores = [
        (
            pltpu.make_async_copy(keys.at[j], ko_hbm.at[j], out_sem.at[0, j]),
            pltpu.make_async_copy(values.at[j], vo_hbm.at[j], out_sem.at[1, j]),
        )
        for j in range(slots)
    ]
    base = lax.axis_index("seq") * slots
    table = table_ref[...]
    code = (
        lax.broadcasted_iota(jnp.int32, table.shape, 0) * most
        + lax.broadcasted_iota(jnp.int32, table.shape, 1)
        + 1
    ).astype(f32)
    owners, starts, lives = [], [], []
    for j in range(slots):
        found = jnp.max(jnp.where(table == base + j, code, 0.0)).astype(jnp.int32)
        place = jnp.maximum(found - 1, 0)
        owner = lax.div(place, most)
        owners.append(owner)
        lives.append(found > 0)
        starts.append(lens_ref[owner] - (place - owner * most) * page)
    wide[...] = jnp.zeros_like(wide)
    acc[...] = jnp.zeros_like(acc)
    at_request = lax.broadcasted_iota(jnp.int32, (requests, block), 0)
    token = lax.broadcasted_iota(jnp.int32, (page, block), 0)
    step_of = lax.div(lax.rem(lax.broadcasted_iota(jnp.int32, (page, block), 1), lines), group)
    ahead = token - step_of
    row = lax.broadcasted_iota(jnp.int32, (page, 1), 0)
    scale = 1.0 / math.sqrt(HD)
    top = jnp.full((requests, block), NEGATIVE, f32)
    for j in range(slots):
        owner, start, live = owners[j], starts[j], lives[j]
        for which, buffer in ((0, keys), (1, values)):
            loads[j][which].wait()

            @pl.when(jnp.logical_and(live, jnp.logical_and(start > -steps, start < page)))
            def _(which=which, buffer=buffer, owner=owner, start=start, j=j):
                value = buffer[j].astype(f32)
                for step in range(steps):
                    fresh = new_ref[which, pl.ds(step * requests + owner, 1), :]
                    value = jnp.where(row == start + step, fresh, value)
                buffer[j] = value.astype(bf16)

            stores[j][which].start()
        query = q_ref[pl.ds(pl.multiple_of(owner * block, block), block), :]
        for k in range(KV):
            wide[j % 2, k * lines : (k + 1) * lines, k * HD : (k + 1) * HD] = query[
                k * lines : (k + 1) * lines
            ]
        score = (
            lax.dot_general(
                keys[j], wide[j % 2], (((1,), (1,)), ((), ())), preferred_element_type=f32
            )
            * scale
        )
        limit = jnp.where(live, start, -2 * page * most)
        score = jnp.where(ahead <= limit, score, NEGATIVE)
        scores[j] = score
        best = jnp.max(score, axis=0, keepdims=True)
        top = jnp.where(at_request == owner, jnp.maximum(top, best), top)
    total = jnp.zeros((requests, block), f32)
    for j in range(slots):
        owner = owners[j]
        best = jnp.max(jnp.where(at_request == owner, top, NEGATIVE), axis=0, keepdims=True)
        score = scores[j]
        prob = jnp.where(score > 0.5 * NEGATIVE, jnp.exp(score - best), 0.0)
        prob = prob.astype(bf16).astype(f32)
        part = jnp.sum(prob, axis=0, keepdims=True)
        total = jnp.where(at_request == owner, total + part, total)
        probs[j] = jnp.transpose(prob).astype(bf16)
    for j in range(slots):
        for k in range(KV):
            part = jnp.dot(
                probs[j, k * lines : (k + 1) * lines, :],
                values[j, :, k * HD : (k + 1) * HD],
                preferred_element_type=f32,
            )
            place = pl.ds(pl.multiple_of(owners[j] * lines, lines), lines)
            acc[k, place, :] += part
    acc_ref[...] = acc[...].astype(bf16)
    stat_ref[...] = jnp.zeros_like(stat_ref)
    for k in range(KV):
        stat_ref[k, :requests, :lines] = top[:, k * lines : (k + 1) * lines]
        stat_ref[k, requests:, :lines] = total[:, k * lines : (k + 1) * lines]
    for store in stores:
        store[0].wait()
        store[1].wait()


def attend(table, lens, q, new, key_cache, value_cache, steps):
    slots, page, width = key_cache.shape
    requests = table.shape[0]
    lines = steps * (H // KV)
    bf16, f32 = jnp.bfloat16, jnp.float32
    vmem = pl.BlockSpec(memory_space=pltpu.VMEM)
    hbm = pl.BlockSpec(memory_space=pl.ANY)
    dma = pltpu.SemaphoreType.DMA
    return pl.pallas_call(
        functools.partial(attend_kernel, steps),
        name="attend",
        out_shape=(
            jax.ShapeDtypeStruct((KV, requests * lines, HD), bf16),
            jax.ShapeDtypeStruct((KV, 2 * requests, 128), f32),
            jax.ShapeDtypeStruct(key_cache.shape, bf16),
            jax.ShapeDtypeStruct(value_cache.shape, bf16),
        ),
        in_specs=[vmem, pl.BlockSpec(memory_space=pltpu.SMEM), vmem, vmem, hbm, hbm],
        out_specs=(vmem, vmem, hbm, hbm),
        scratch_shapes=[
            pltpu.VMEM(key_cache.shape, bf16),
            pltpu.VMEM(value_cache.shape, bf16),
            pltpu.VMEM((2, KV * lines, width), bf16),
            pltpu.VMEM((slots, page, KV * lines), f32),
            pltpu.VMEM((slots, KV * lines, page), bf16),
            pltpu.VMEM((KV, requests * lines, HD), f32),
            dma((2, slots)),
            dma((2, slots)),
        ],
        compiler_params=pltpu.CompilerParams(vmem_limit_bytes=32 * 2**20),
    )(table, lens, q, new, key_cache, value_cache)


def merge_kernel(
    zs,
    ss,
    acc_ref,
    stat_ref,
    x_ref,
    w_hbm,
    out_ref,
    w,
    acc,
    stat,
    got,
    got_stat,
    mixed,
    heads,
    everyone,
    joined,
    w_sem,
    a_send,
    a_recv,
    b_send,
    b_recv,
):
    z = lax.axis_index("req")
    s = lax.axis_index("seq")
    f32 = jnp.float32
    rows = x_ref.shape[0]
    per = H // ss
    parts = 4
    depth = D // parts
    loads = [
        pltpu.make_async_copy(
            w_hbm.at[pl.ds(part * depth, depth)], w.at[pl.ds(part * depth, depth)], w_sem.at[part]
        )
        for part in range(parts)
    ]
    for load in loads:
        load.start()
    partners = [{"req": z, "seq": lax.rem(s + k, ss)} for k in range(1, ss)]
    acc[...] = acc_ref[...]
    stat[...] = stat_ref[...]
    greet(partners)
    first = []
    for k in range(1, ss):
        to = lax.rem(s + k, ss)
        first.append(
            remote(stat.at[to], got_stat.at[s], a_send.at[1, k], a_recv.at[1, k], partners[k - 1])
        )
        first.append(
            remote(acc.at[to], got.at[s], a_send.at[0, k], a_recv.at[0, k], partners[k - 1])
        )
    for copy in first:
        copy.start()
    got[s] = acc[s]
    got_stat[s] = stat[s]
    for copy in first:
        copy.wait_recv()
    requests = stat.shape[1] // 2
    lines = rows // requests * per
    best = got_stat[0, :requests]
    for other in range(1, ss):
        best = jnp.maximum(best, got_stat[other, :requests])
    shares = [jnp.exp(got_stat[other, :requests] - best) for other in range(ss)]
    denominator = shares[0] * got_stat[0, requests:]
    for other in range(1, ss):
        denominator = denominator + shares[other] * got_stat[other, requests:]
    lane = lax.broadcasted_iota(jnp.int32, denominator.shape, 1)
    denominator = jnp.where(lane < lines, denominator, 1.0)
    tall = jnp.transpose(jnp.concatenate([share / denominator for share in shares], axis=0))
    for request in range(requests):
        span = slice(request * lines, (request + 1) * lines)
        value = got[0, span, :].astype(f32) * tall[:lines, request : request + 1]
        for other in range(1, ss):
            at = other * requests + request
            value = value + got[other, span, :].astype(f32) * tall[:lines, at : at + 1]
        mixed[span, :] = value
    for head in range(per):
        for step in range(rows // requests):
            heads[step * requests : (step + 1) * requests, head * HD : (head + 1) * HD] = mixed[
                pl.ds(step * per + head, requests, stride=lines), :
            ].astype(jnp.bfloat16)
    second = [
        remote(heads, everyone.at[s], b_send.at[k], b_recv.at[k], partners[k - 1])
        for k in range(1, ss)
    ]
    for copy in second:
        copy.start()
    everyone[s] = heads[...]
    for copy in second:
        copy.wait_recv()
    for other in range(ss):
        joined[:, other * per * HD : (other + 1) * per * HD] = everyone[other]
    result = x_ref[...].astype(f32)
    for part in range(parts):
        loads[part].wait()
        span = slice(part * depth, (part + 1) * depth)
        result += jnp.dot(joined[:, span], w[span, :], preferred_element_type=f32)
    out_ref[...] = result.astype(jnp.bfloat16)
    for copy in first + second:
        copy.wait_send()


def merge(acc, stat, x, w, zs, ss):
    rows, features = x.shape
    bf16, f32 = jnp.bfloat16, jnp.float32
    vmem = pl.BlockSpec(memory_space=pltpu.VMEM)
    dma = pltpu.SemaphoreType.DMA
    return pl.pallas_call(
        functools.partial(merge_kernel, zs, ss),
        name="merge",
        out_shape=jax.ShapeDtypeStruct((rows, features), bf16),
        in_specs=[vmem, vmem, vmem, pl.BlockSpec(memory_space=pl.ANY)],
        out_specs=vmem,
        scratch_shapes=[
            pltpu.VMEM(w.shape, bf16),
            pltpu.VMEM(acc.shape, bf16),
            pltpu.VMEM(stat.shape, f32),
            pltpu.VMEM(acc.shape, bf16),
            pltpu.VMEM(stat.shape, f32),
            pltpu.VMEM(acc.shape[1:], f32),
            pltpu.VMEM((rows, H // ss * HD), bf16),
            pltpu.VMEM((ss, rows, H // ss * HD), bf16),
            pltpu.VMEM((rows, H * HD), bf16),
            dma((4,)),
            dma((2, ss)),
            dma((2, ss)),
            dma((ss,)),
            dma((ss,)),
        ],
        compiler_params=pltpu.CompilerParams(
            collective_id=2, has_side_effects=True, vmem_limit_bytes=48 * 2**20
        ),
    )(acc, stat, x, w)


def on_device(
    hidden_in,
    cache_lens,
    page_table,
    key_cache,
    value_cache,
    norm_attn,
    w_qkv,
    b_qkv,
    w_out,
    norm_mlp,
    w_gate,
    w_up,
    w_down,
):
    steps, requests, blocks, pieces = hidden_in.shape
    rows = steps * requests
    group = H // KV
    quarter = D // blocks
    seq = quarter // pieces
    zs = D // w_gate.shape[0]
    fast = (
        pieces % 128 == 0
        and w_qkv.shape[1] % 128 == 0
        and zs == blocks
        and zs % 2 == 0
        and rows <= 128
        and rows % 16 == 0
        and requests == 8
        and seq == KV
    )
    lines = steps * group
    if fast:
        queries, fresh = project(
            cache_lens,
            hidden_in.reshape(rows, blocks * pieces),
            norm_attn.reshape(-1, 128),
            b_qkv.reshape(1, -1),
            w_qkv,
            zs,
            seq,
            steps,
        )
    else:
        flat = (
            lax.all_gather(hidden_in, "seq", axis=3, tiled=True).reshape(rows, D).astype(jnp.float32)
        )
        normed = (
            flat * lax.rsqrt(jnp.mean(flat * flat, axis=1, keepdims=True) + EPSILON) * norm_attn
        ).astype(jnp.bfloat16)
        columns = (
            jnp.dot(normed, w_qkv, preferred_element_type=jnp.float32) + b_qkv.astype(jnp.float32)
        ).astype(jnp.bfloat16)
        projected = lax.all_gather(columns, "seq", axis=1, tiled=True)
        position = (
            jnp.arange(steps, dtype=jnp.int32)[:, None] + cache_lens[None, :]
        ).reshape(rows)
        rotated = rotate(
            projected[:, : (H + KV) * HD].reshape(rows, H + KV, HD).astype(jnp.float32), position
        ).astype(jnp.bfloat16)
        queries = jnp.transpose(
            rotated[:, :H].reshape(steps, requests, KV, group, HD), (1, 2, 0, 3, 4)
        ).reshape(rows * H, HD)
        fresh = jnp.stack(
            [rotated[:, H:].reshape(rows, KV * HD), projected[:, (H + KV) * HD :]]
        ).astype(jnp.float32)
    weighted, stat, key_cache, value_cache = attend(
        page_table, cache_lens, queries, fresh, key_cache, value_cache, steps
    )

    if fast:
        middle = merge(
            weighted,
            stat,
            hidden_in.reshape(rows, blocks * pieces),
            w_out.reshape(H * HD, blocks * pieces),
            zs,
            seq,
        )
    else:

        def by_head(value):
            value = jnp.moveaxis(value.reshape((KV, requests, steps, group) + value.shape[2:]), 1, 3)
            value = jnp.swapaxes(value, 1, 2)
            return value.reshape(seq, -1)

        def by_line(value):
            return by_head(value[:, :, :lines].reshape(KV, requests * lines))

        packed = jnp.concatenate(
            [
                by_head(weighted.astype(jnp.float32)),
                by_line(stat[:, :requests]),
                by_line(stat[:, requests:]),
            ],
            axis=1,
        )
        packed = lax.all_to_all(packed, "seq", split_axis=0, concat_axis=0, tiled=True)
        count = (H // seq) * rows
        part_acc = packed[:, : count * HD].reshape(seq, count, HD)
        part_top = packed[:, count * HD : count * (HD + 1)]
        part_sum = packed[:, count * (HD + 1) :]
        best = jnp.max(part_top, axis=0)
        share = jnp.exp(part_top - best[None])
        denominator = jnp.sum(share * part_sum, axis=0)
        numerator = jnp.sum(share[..., None] * part_acc, axis=0)
        heads = (numerator / denominator[:, None]).astype(jnp.bfloat16)
        heads = jnp.swapaxes(heads.reshape(H // seq, rows, HD), 0, 1).reshape(rows, -1)
        attended = lax.all_gather(heads, "seq", axis=1, tiled=True)
        branch_out = jnp.dot(
            attended, w_out.reshape(H * HD, blocks * pieces), preferred_element_type=jnp.float32
        ).reshape(rows, blocks, pieces)
        current = hidden_in.reshape(rows, blocks, pieces).astype(jnp.float32)
        middle = (current + branch_out).astype(jnp.bfloat16)
    if fast:
        gain = lax.dynamic_slice(norm_mlp, (lax.axis_index("req") * quarter,), (quarter,))
        output = mlp(
            middle.reshape(rows, blocks * pieces),
            gain.reshape(1, quarter),
            jnp.swapaxes(w_gate, 0, 1),
            jnp.swapaxes(w_up, 0, 1),
            w_down,
            zs,
            seq,
        )
        return (output.reshape(hidden_in.shape), key_cache, value_cache)
    rows_mid = lax.all_gather(middle, "seq", axis=2, tiled=True).astype(jnp.float32)
    inverse = lax.rsqrt(jnp.mean(rows_mid * rows_mid, axis=(1, 2), keepdims=True) + EPSILON)
    normed_mid = (rows_mid * inverse * norm_mlp.reshape(blocks, quarter)).astype(jnp.bfloat16)
    mine = lax.all_to_all(normed_mid, "req", split_axis=1, concat_axis=0, tiled=True).reshape(
        -1, quarter
    )
    gate_part = jnp.dot(mine, w_gate, preferred_element_type=jnp.float32).astype(jnp.bfloat16)
    up_part = jnp.dot(mine, w_up, preferred_element_type=jnp.float32).astype(jnp.bfloat16)
    gate_sum = lax.psum_scatter(gate_part, "req", scatter_dimension=0, tiled=True)
    up_sum = lax.psum_scatter(up_part, "req", scatter_dimension=0, tiled=True)
    hidden_part = (
        jax.nn.silu(gate_sum.astype(jnp.float32)) * up_sum.astype(jnp.float32)
    ).astype(jnp.bfloat16)
    hidden = lax.all_gather(hidden_part, "req", axis=0, tiled=True)
    down = jnp.dot(hidden, w_down, preferred_element_type=jnp.float32)
    sums = lax.psum_scatter(
        down.reshape(down.shape[0], 1, quarter).astype(jnp.bfloat16),
        "seq",
        scatter_dimension=2,
        tiled=True,
    ).astype(jnp.float32)
    back = lax.all_to_all(sums, "req", split_axis=0, concat_axis=1, tiled=True)
    output = (middle.astype(jnp.float32) + back).astype(jnp.bfloat16)
    return (output.reshape(hidden_in.shape), key_cache, value_cache)


def solution(mesh):
    in_specs = (
        P(None, "req", None, "seq"),
        P("req"),
        P("req", None),
        P(("req", "seq"), None, None),
        P(("req", "seq"), None, None),
        P(),
        P(None, "seq"),
        P("seq"),
        P(None, None, "seq"),
        P(),
        P("req", "seq"),
        P("req", "seq"),
        P("seq", "req"),
    )
    out_specs = (
        P(None, "req", None, "seq"),
        P(("req", "seq"), None, None),
        P(("req", "seq"), None, None),
    )
    return jax.shard_map(
        on_device, mesh=mesh, in_specs=in_specs, out_specs=out_specs, check_vma=False
    )
```

```python
import functools
import math

import jax
import jax.numpy as jnp
from jax import lax
from jax.experimental import pallas as pl
from jax.experimental.pallas import tpu as pltpu
from jax.sharding import PartitionSpec as P

D = 8192
H = 64
KV = 8
HD = 128
STEPS = 4


EPSILON = 1e-06
THETA = 1000000.0
NEGATIVE = -1e30


def rotate(heads, position):
    half = heads.shape[-1] // 2
    freq = THETA ** (-(jnp.arange(half, dtype=jnp.float32) * 2.0 / heads.shape[-1]))
    angle = position.astype(jnp.float32)[:, None, None] * freq[None, None, :]
    cosine = jnp.cos(angle)
    sine = jnp.sin(angle)
    first = heads[..., :half]
    second = heads[..., half:]
    return jnp.concatenate(
        [first * cosine - second * sine, second * cosine + first * sine], axis=-1
    )


MESH = pl.DeviceIdType.MESH


def greet(partners):
    barrier = pltpu.get_barrier_semaphore()
    for partner in partners:
        pl.semaphore_signal(barrier, inc=1, device_id=partner, device_id_type=MESH)
    pl.semaphore_wait(barrier, len(partners))


def remote(src, dst, send, recv, partner):
    return pltpu.make_async_remote_copy(
        src_ref=src,
        dst_ref=dst,
        send_sem=send,
        recv_sem=recv,
        device_id=partner,
        device_id_type=MESH,
    )


class Gather:
    def __init__(self, z, s, ss, dst, send, recv):
        def flip(value, bit):
            return value + bit - 2 * bit * lax.rem(lax.div(value, bit), 2)

        self.twin = flip(s, 1)
        self.peers = []
        for mask in range(1, ss // 2):
            value, bit = s, 2
            while bit < ss:
                if mask & (bit // 2):
                    value = flip(value, bit)
                bit *= 2
            self.peers.append(value)
        count = len(self.peers)
        self.slots = (
            [s, self.twin] + self.peers + [flip(peer, 1) for peer in self.peers]
        )
        twin = {"req": z, "seq": self.twin}
        self.partners = [twin] + [{"req": z, "seq": peer} for peer in self.peers]
        self.parts = list(zip(dst, send, recv))
        self.direct, self.onward = [], []
        for i, partner in enumerate(self.partners):
            self.direct.append(
                [remote(d.at[s], d.at[s], a.at[i], b.at[i], partner) for d, a, b in self.parts]
            )
        for i, peer in enumerate(self.peers):
            at = count + 1 + i
            self.onward.append(
                [remote(d.at[peer], d.at[peer], a.at[at], b.at[at], twin) for d, a, b in self.parts]
            )

    def start(self):
        for copies in self.direct:
            for copy in copies:
                copy.start()

    def wait(self, step):
        if step == 0:
            return
        if step <= len(self.direct):
            for copy in self.direct[step - 1]:
                copy.wait_recv()
            if step > 1:
                for copy in self.onward[step - 2]:
                    copy.start()
        else:
            for copy in self.onward[step - 1 - len(self.direct)]:
                copy.wait_recv()

    def wait_all(self):
        for step in range(len(self.slots)):
            self.wait(step)

    def wait_sent(self):
        for copies in self.direct + self.onward:
            for copy in copies:
                copy.wait_send()


WIDTH = 256
LAGS = (0, 2, 4, 7, 10, 12, 14)
RING = 8
KEPT = 4


def tail_kernel(
    zs,
    ss,
    width,
    acc_ref,
    stat_ref,
    x_ref,
    norm_ref,
    wo_hbm,
    wg_hbm,
    wu_hbm,
    wd_hbm,
    out_ref,
    wo,
    wg,
    wu,
    wd,
    got_acc,
    got_stat,
    mixed,
    everyone,
    pick,
    mid,
    cut,
    square,
    got,
    got_sq,
    normed,
    own_g,
    own_u,
    send_r,
    recv_r,
    send_l,
    recv_l,
    hid,
    down,
    parts,
    landed,
    sums,
    back,
    wo_sem,
    w_sem,
    wd_sem,
    m_send,
    m_recv,
    h_send,
    h_recv,
    a_send,
    a_recv,
    b_send,
    b_recv,
    rs_send,
    rs_recv,
    ag_send,
    ag_recv,
    d_send,
    d_recv,
    e_send,
    e_recv,
):
    z = lax.axis_index("req")
    s = lax.axis_index("seq")
    f32, bf16 = jnp.float32, jnp.bfloat16
    rows, features = x_ref.shape
    pieces = features // zs
    per = H // ss
    units = wg.shape[0]
    half = zs * rows // 2
    starts = list(range(0, units, width))
    count = len(starts)
    sizes = [min(width, units - start) for start in starts]
    padded = [-(-size // 128) * 128 for size in sizes]
    z_partners = [{"req": lax.rem(z + k, zs), "seq": s} for k in range(1, zs)]
    s_partners = [{"req": z, "seq": lax.rem(s + k, ss)} for k in range(1, ss)]
    attended = Gather(z, s, ss, [everyone], [h_send], [h_recv])
    depth = D // ss

    def wo_load(n):
        first_row = pl.multiple_of(attended.slots[n] * depth, depth)
        return pltpu.make_async_copy(
            wo_hbm.at[pl.ds(first_row, depth)], wo.at[n % KEPT], wo_sem.at[n % KEPT]
        )

    def wd_load(p):
        return pltpu.make_async_copy(
            wd_hbm.at[pl.ds(starts[p], sizes[p])],
            wd.at[p % RING, pl.ds(0, sizes[p])],
            wd_sem.at[p % RING],
        )

    g_load = pltpu.make_async_copy(wg_hbm, wg, w_sem.at[0])
    u_load = pltpu.make_async_copy(wu_hbm, wu, w_sem.at[1])
    for n in range(KEPT):
        wo_load(n).start()
    g_load.start()
    greet(z_partners + s_partners)

    first = []
    for k in range(1, ss):
        to = lax.rem(s + k, ss)
        first.append(
            remote(stat_ref.at[to], got_stat.at[s], m_send.at[1, k], m_recv.at[1, k], s_partners[k - 1])
        )
        first.append(
            remote(acc_ref.at[to], got_acc.at[s], m_send.at[0, k], m_recv.at[0, k], s_partners[k - 1])
        )
    for copy in first:
        copy.start()
    got_acc[s] = acc_ref[s]
    got_stat[s] = stat_ref[s]
    span = zs * 256
    pick[...] = jnp.where(
        lax.div(lax.broadcasted_iota(jnp.int32, (256, span), 1), zs)
        == lax.broadcasted_iota(jnp.int32, (256, span), 0),
        1.0,
        0.0,
    ).astype(bf16)
    for copy in first:
        copy.wait_recv()
    u_load.start()
    requests = stat_ref.shape[1] // 2
    lines = rows // requests * per
    best = got_stat[0, :requests]
    for other in range(1, ss):
        best = jnp.maximum(best, got_stat[other, :requests])
    shares = [jnp.exp(got_stat[other, :requests] - best) for other in range(ss)]
    denominator = shares[0] * got_stat[0, requests:]
    for other in range(1, ss):
        denominator = denominator + shares[other] * got_stat[other, requests:]
    lane = lax.broadcasted_iota(jnp.int32, denominator.shape, 1)
    denominator = jnp.where(lane < lines, denominator, 1.0)
    tall = jnp.transpose(jnp.concatenate([share / denominator for share in shares], axis=0))
    for request in range(requests):
        place = slice(request * lines, (request + 1) * lines)
        value = got_acc[0, place, :].astype(f32) * tall[:lines, request : request + 1]
        for other in range(1, ss):
            at = other * requests + request
            value = value + got_acc[other, place, :].astype(f32) * tall[:lines, at : at + 1]
        mixed[place, :] = value
    for head in range(per):
        column = [
            mixed[pl.ds(step * per + head, requests, stride=lines), :]
            for step in range(rows // requests)
        ]
        everyone[s, :, head * HD : (head + 1) * HD] = jnp.concatenate(column, axis=0).astype(bf16)
    attended.start()

    which = lax.rem(lax.broadcasted_iota(jnp.int32, (rows, span), 1), zs)
    result = jnp.zeros((zs * rows, pieces), f32)
    for n in range(ss):
        attended.wait(n)
        block = everyone[attended.slots[n]]
        chunks = depth // 256
        tower = jnp.concatenate([block[:, c * 256 : (c + 1) * 256] for c in range(chunks)], axis=0)
        spread = jnp.dot(tower, pick[...], preferred_element_type=f32)
        wo_load(n).wait()
        for c in range(chunks):
            line = spread[c * rows : (c + 1) * rows]
            left = jnp.concatenate(
                [jnp.where(which == b, line, 0.0) for b in range(zs)], axis=0
            ).astype(bf16)
            right = wo[n % KEPT, c * 256 : (c + 1) * 256].reshape(span, pieces)
            result = result + jnp.dot(left, right, preferred_element_type=f32)
        if n + KEPT < ss:
            wo_load(n + KEPT).start()
    for p in range(min(RING, count)):
        wd_load(p).start()
    total = jnp.zeros((8, rows), f32)
    for block in range(zs):
        cols = slice(block * pieces, (block + 1) * pieces)
        piece = (
            x_ref[:, cols].astype(f32) + result[block * rows : (block + 1) * rows]
        ).astype(bf16)
        mid[:, cols] = piece
        cut[block] = piece
        value = piece.astype(f32)
        total += lax.dot_general(
            jnp.ones((8, pieces), f32),
            value * value,
            (((1,), (1,)), ((), ())),
            precision=lax.Precision.HIGHEST,
            preferred_element_type=f32,
        )
    square[...] = jnp.zeros_like(square)
    square[:, :rows] = total
    second = []
    for k in range(1, zs):
        to = lax.rem(z + k, zs)
        second.append(
            remote(cut.at[to], got.at[s, z], a_send.at[0, k], a_recv.at[0, k], z_partners[k - 1])
        )
        second.append(
            remote(square, got_sq.at[s, z], a_send.at[1, k], a_recv.at[1, k], z_partners[k - 1])
        )
    for copy in second:
        copy.start()
    got[s, z] = cut[z]
    got_sq[s, z] = square[...]
    for copy in second:
        copy.wait_recv()
    blocks = Gather(z, s, ss, [got, got_sq], [b_send.at[0], b_send.at[1]], [b_recv.at[0], b_recv.at[1]])
    blocks.start()
    if sizes[-1] != padded[-1]:
        send_r[count - 1] = jnp.zeros_like(send_r[count - 1])
        send_l[count - 1] = jnp.zeros_like(send_l[count - 1])
        hid[count - 1] = jnp.zeros_like(hid[count - 1])
    down[...] = jnp.zeros_like(down)
    blocks.wait_all()
    for group in range(zs):
        line = got_sq[0, group]
        for other in range(1, ss):
            line = line + got_sq[other, group]
        spread = lax.dot_general(
            line[:, :rows],
            jnp.full((8, 128), 0.125, f32),
            (((0,), (0,)), ((), ())),
            precision=lax.Precision.HIGHEST,
            preferred_element_type=f32,
        )
        inverse = lax.rsqrt(spread / D + EPSILON)
        for other in range(ss):
            for part in range(pieces // 128):
                at = other * pieces + part * 128
                gain = norm_ref[pl.ds(z * (ss * pieces // 128) + at // 128, 1), :]
                value = got[other, group, :, part * 128 : (part + 1) * 128].astype(f32)
                normed[group * rows : (group + 1) * rows, at : at + 128] = (
                    value * inverse * gain
                ).astype(bf16)
    g_load.wait()
    u_load.wait()

    right = {"req": lax.rem(z + 1, zs), "seq": s}
    left = {"req": lax.rem(z + zs - 1, zs), "seq": s}

    def reduce_copy(way, p):
        src, dst, to = ((send_r, recv_r, right), (send_l, recv_l, left))[way]
        lanes = pl.ds(0, 2 * padded[p])
        return remote(
            src.at[p, :, lanes], dst.at[p, :, lanes], rs_send.at[way, p], rs_recv.at[way, p], to
        )

    def hidden_copy(way, p):
        place = (p, pl.ds(half * (1 - way), half), pl.ds(0, padded[p]))
        return remote(
            hid.at[place],
            hid.at[place],
            ag_send.at[way, p],
            ag_recv.at[way, p],
            (left, right)[way],
        )

    def reduce_step(way, p, place):
        size, pad = sizes[p], padded[p]
        base = half * (1 - way)
        cols = slice(starts[p], starts[p] + size)
        gate = own_g[base : base + half, cols]
        up = own_u[base : base + half, cols]
        if place > 0:
            reduce_copy(way, p).wait_recv()
            came = (recv_r, recv_l)[way]
            gate = gate + came[p, :, :size].astype(f32)
            up = up + came[p, :, pad : pad + size].astype(f32)
        if place < zs - 1:
            goes = (send_r, send_l)[way]
            goes[p, :, :size] = gate.astype(bf16)
            goes[p, :, pad : pad + size] = up.astype(bf16)
            reduce_copy(way, p).start()
        else:
            gate = gate.astype(bf16).astype(f32)
            up = up.astype(bf16).astype(f32)
            hid[p, base : base + half, :size] = (gate / (1.0 + jnp.exp(-gate)) * up).astype(bf16)
            hidden_copy(way, p).start()

    def down_step(p):
        wd_load(p).wait()
        down[...] += jnp.dot(
            hid[p, :, : sizes[p]], wd[p % RING, : sizes[p], :], preferred_element_type=f32
        )
        if p + RING < count:
            wd_load(p + RING).start()

    nt = (((1,), (1,)), ((), ()))
    lag = LAGS if zs == 4 else tuple(2 * i for i in range(2 * zs - 1))
    last = lag[2 * zs - 2]
    for i in range(count + last):
        if i < count:
            cols = slice(starts[i], starts[i] + sizes[i])
            own_g[:, cols] = lax.dot_general(normed[...], wg[cols, :], nt, preferred_element_type=f32)
            own_u[:, cols] = lax.dot_general(normed[...], wu[cols, :], nt, preferred_element_type=f32)
        for zz in range(zs):

            @pl.when(z == zz)
            def _(zz=zz, i=i):
                order = (0, 1) if zz < zs // 2 else (1, 0)
                for way in order:
                    place = zz if way == 0 else zs - 1 - zz
                    p = i - lag[place]
                    if 0 <= p < count:
                        reduce_step(way, p, place)
                for way in order[::-1]:
                    place = zs - 1 - zz if way == 0 else zz
                    p = i - lag[zs - 1 + place]
                    if place > 0 and 0 <= p < count:
                        hidden_copy(way, p).wait_recv()
                        if place < zs - 1:
                            hidden_copy(way, p).start()

        if i >= last:
            down_step(i - last)

    for other in range(ss):
        parts[other] = down[:, other * pieces : (other + 1) * pieces].astype(bf16)
    third = []
    for k in range(1, ss):
        to = lax.rem(s + k, ss)
        third.append(
            remote(parts.at[to], landed.at[s], d_send.at[k], d_recv.at[k], s_partners[k - 1])
        )
    for copy in third:
        copy.start()
    landed[s] = parts[s]
    for copy in third:
        copy.wait_recv()
    whole = landed[0].astype(f32)
    for other in range(1, ss):
        whole = whole + landed[other].astype(f32)
    for group in range(zs):
        sums[group] = whole[group * rows : (group + 1) * rows]
    fourth = []
    for k in range(1, zs):
        to = lax.rem(z + k, zs)
        fourth.append(
            remote(sums.at[to], back.at[z], e_send.at[k], e_recv.at[k], z_partners[k - 1])
        )
    for copy in fourth:
        copy.start()
    back[z] = sums[z]
    for copy in fourth:
        copy.wait_recv()
    for block in range(zs):
        cols = slice(block * pieces, (block + 1) * pieces)
        out_ref[:, cols] = (mid[:, cols].astype(f32) + back[block]).astype(bf16)

    for copy in first + second + third + fourth:
        copy.wait_send()
    attended.wait_sent()
    blocks.wait_sent()
    for way in range(2):
        for p in range(count):

            @pl.when(z != (zs - 1 if way == 0 else 0))
            def _(way=way, p=p):
                reduce_copy(way, p).wait_send()

            @pl.when(z != (0 if way == 0 else zs - 1))
            def _(way=way, p=p):
                hidden_copy(way, p).wait_send()


def tail(acc, stat, x, norm, w_out, w_gate, w_up, w_down, zs, ss):
    rows, features = x.shape
    pieces = features // zs
    units, depth = w_gate.shape
    quarter = w_down.shape[1]
    width = WIDTH
    count = -(-units // width)
    everyone = zs * rows
    half = everyone // 2
    bf16, f32 = jnp.bfloat16, jnp.float32
    vmem = pl.BlockSpec(memory_space=pltpu.VMEM)
    hbm = pl.BlockSpec(memory_space=pl.ANY)
    dma = pltpu.SemaphoreType.DMA
    return pl.pallas_call(
        functools.partial(tail_kernel, zs, ss, width),
        name="tail",
        out_shape=jax.ShapeDtypeStruct(x.shape, bf16),
        in_specs=[vmem, vmem, vmem, vmem, hbm, hbm, hbm, hbm],
        out_specs=vmem,
        scratch_shapes=[
            pltpu.VMEM((KEPT, D // ss) + w_out.shape[1:], bf16),
            pltpu.VMEM(w_gate.shape, bf16),
            pltpu.VMEM(w_up.shape, bf16),
            pltpu.VMEM((RING, width, quarter), bf16),
            pltpu.VMEM(acc.shape, bf16),
            pltpu.VMEM(stat.shape, f32),
            pltpu.VMEM(acc.shape[1:], f32),
            pltpu.VMEM((ss, rows, H // ss * HD), bf16),
            pltpu.VMEM((256, zs * 256), bf16),
            pltpu.VMEM((rows, features), bf16),
            pltpu.VMEM((zs, rows, pieces), bf16),
            pltpu.VMEM((8, 128), f32),
            pltpu.VMEM((ss, zs, rows, pieces), bf16),
            pltpu.VMEM((ss, zs, 8, 128), f32),
            pltpu.VMEM((everyone, depth), bf16),
            pltpu.VMEM((everyone, units), f32),
            pltpu.VMEM((everyone, units), f32),
            pltpu.VMEM((count, half, 2 * width), bf16),
            pltpu.VMEM((count, half, 2 * width), bf16),
            pltpu.VMEM((count, half, 2 * width), bf16),
            pltpu.VMEM((count, half, 2 * width), bf16),
            pltpu.VMEM((count, everyone, width), bf16),
            pltpu.VMEM((everyone, quarter), f32),
            pltpu.VMEM((ss, everyone, pieces), bf16),
            pltpu.VMEM((ss, everyone, pieces), bf16),
            pltpu.VMEM((zs, rows, pieces), f32),
            pltpu.VMEM((zs, rows, pieces), f32),
            dma((KEPT,)),
            dma((2,)),
            dma((RING,)),
            dma((2, ss)),
            dma((2, ss)),
            dma((ss,)),
            dma((ss,)),
            dma((2, zs)),
            dma((2, zs)),
            dma((2, ss)),
            dma((2, ss)),
            dma((2, count)),
            dma((2, count)),
            dma((2, count)),
            dma((2, count)),
            dma((ss,)),
            dma((ss,)),
            dma((zs,)),
            dma((zs,)),
        ],
        compiler_params=pltpu.CompilerParams(
            collective_id=0, has_side_effects=True, vmem_limit_bytes=63 * 2**20
        ),
    )(acc, stat, x, norm, w_out, w_gate, w_up, w_down)


def project_kernel(
    zs,
    ss,
    steps,
    lens_ref,
    x_ref,
    norm_ref,
    bias_ref,
    w_hbm,
    q_ref,
    new_ref,
    w,
    got,
    normed,
    columns,
    spread,
    w_sem,
    a_send,
    a_recv,
    b_send,
    b_recv,
):
    z = lax.axis_index("req")
    s = lax.axis_index("seq")
    f32 = jnp.float32
    rows, features = x_ref.shape
    requests = rows // steps
    blocks = zs
    pieces = features // blocks
    mine = w.shape[1]
    local = mine // HD
    group = H // KV
    parts = 4
    depth = D // parts
    loads = [
        pltpu.make_async_copy(
            w_hbm.at[pl.ds(part * depth, depth)], w.at[pl.ds(part * depth, depth)], w_sem.at[part]
        )
        for part in range(parts)
    ]
    for load in loads:
        load.start()
    inputs = Gather(z, s, ss, [got], [a_send], [a_recv])
    outputs = Gather(z, s, ss, [columns], [b_send], [b_recv])
    got[s] = x_ref[...]
    greet(inputs.partners)
    inputs.start()
    row = lax.broadcasted_iota(jnp.int32, (rows, HD), 0)
    position = lax.div(row, requests)
    for request in range(requests):
        position = position + jnp.where(lax.rem(row, requests) == request, lens_ref[request], 0)
    lane = lax.broadcasted_iota(jnp.int32, (rows, HD), 1)
    entry = lax.rem(lane, HD // 2).astype(f32)
    angle = position.astype(f32) * jnp.exp(entry * (-2.0 * math.log(THETA) / HD))
    cosine = jnp.cos(angle)
    sine = jnp.where(lane < HD // 2, -jnp.sin(angle), jnp.sin(angle))
    inputs.wait_all()
    total = jnp.zeros((rows, 1), f32)
    for other in range(ss):
        value = got[other].astype(f32)
        total += jnp.sum(value * value, axis=1, keepdims=True)
    inverse = lax.rsqrt(total / D + EPSILON)
    for other in range(ss):
        for block in range(blocks):
            base = block * ss * pieces + other * pieces
            for line in range(pieces // 128):
                at = base + line * 128
                value = got[
                    other, :, block * pieces + line * 128 : block * pieces + (line + 1) * 128
                ].astype(f32)
                gain = norm_ref[at // 128 : at // 128 + 1, :]
                normed[:, at : at + 128] = (value * inverse * gain).astype(jnp.bfloat16)
    result = jnp.zeros((rows, mine), f32)
    for part in range(parts):
        loads[part].wait()
        span = slice(part * depth, (part + 1) * depth)
        result += jnp.dot(normed[:, span], w[span, :], preferred_element_type=f32)
    result = (result + bias_ref[...].astype(f32)).astype(jnp.bfloat16).astype(f32)
    for head in range(local):
        tile = result[:, head * HD : (head + 1) * HD]
        turned = tile * cosine + pltpu.roll(tile, HD // 2, axis=1) * sine
        columns[s, :, head * HD : (head + 1) * HD] = jnp.where(
            s * local + head < H + KV, turned, tile
        ).astype(jnp.bfloat16)
    outputs.start()
    outputs.wait_all()
    for head in range(H + 2 * KV):
        other, at = head // local, (head % local) * HD
        tile = columns[other, :, at : at + HD].astype(f32)
        if head < H:
            for step in range(steps):
                base = (head // group) * steps * group + step * group + head % group
                spread[pl.ds(base, requests, stride=H * steps), :] = tile[
                    step * requests : (step + 1) * requests
                ]
        else:
            at = ((head - H) % KV) * HD
            new_ref[(head - H) // KV, :, at : at + HD] = tile
    q_ref[...] = spread[...].astype(jnp.bfloat16)
    inputs.wait_sent()
    outputs.wait_sent()


def project(lens, x, norm, bias, w, zs, ss, steps):
    rows, features = x.shape
    mine = w.shape[1]
    bf16, f32 = jnp.bfloat16, jnp.float32
    vmem = pl.BlockSpec(memory_space=pltpu.VMEM)
    dma = pltpu.SemaphoreType.DMA
    return pl.pallas_call(
        functools.partial(project_kernel, zs, ss, steps),
        name="project",
        out_shape=(
            jax.ShapeDtypeStruct((rows * H, HD), bf16),
            jax.ShapeDtypeStruct((2, rows, KV * HD), f32),
        ),
        in_specs=[
            pl.BlockSpec(memory_space=pltpu.SMEM),
            vmem,
            vmem,
            vmem,
            pl.BlockSpec(memory_space=pl.ANY),
        ],
        out_specs=(vmem, vmem),
        scratch_shapes=[
            pltpu.VMEM(w.shape, bf16),
            pltpu.VMEM((ss, rows, features), bf16),
            pltpu.VMEM((rows, D), bf16),
            pltpu.VMEM((ss, rows, mine), bf16),
            pltpu.VMEM((rows * H, HD), f32),
            dma((4,)),
            dma((ss,)),
            dma((ss,)),
            dma((ss,)),
            dma((ss,)),
        ],
        compiler_params=pltpu.CompilerParams(
            collective_id=1, has_side_effects=True, vmem_limit_bytes=48 * 2**20
        ),
    )(lens, x, norm, bias, w)


def attend_kernel(
    steps,
    table_ref,
    lens_ref,
    q_ref,
    new_ref,
    k_hbm,
    v_hbm,
    acc_ref,
    stat_ref,
    ko_hbm,
    vo_hbm,
    keys,
    values,
    wide,
    scores,
    probs,
    acc,
    in_sem,
    out_sem,
):
    f32, bf16 = jnp.float32, jnp.bfloat16
    slots, page, _ = keys.shape
    requests, most = table_ref.shape
    group = H // KV
    lines = steps * group
    block = KV * lines
    loads = [
        (
            pltpu.make_async_copy(k_hbm.at[j], keys.at[j], in_sem.at[0, j]),
            pltpu.make_async_copy(v_hbm.at[j], values.at[j], in_sem.at[1, j]),
        )
        for j in range(slots)
    ]
    for load in loads:
        load[0].start()
    for load in loads:
        load[1].start()
    stores = [
        (
            pltpu.make_async_copy(keys.at[j], ko_hbm.at[j], out_sem.at[0, j]),
            pltpu.make_async_copy(values.at[j], vo_hbm.at[j], out_sem.at[1, j]),
        )
        for j in range(slots)
    ]
    base = lax.axis_index("seq") * slots
    table = table_ref[...]
    code = (
        lax.broadcasted_iota(jnp.int32, table.shape, 0) * most
        + lax.broadcasted_iota(jnp.int32, table.shape, 1)
        + 1
    ).astype(f32)
    owners, starts, lives = [], [], []
    for j in range(slots):
        found = jnp.max(jnp.where(table == base + j, code, 0.0)).astype(jnp.int32)
        place = jnp.maximum(found - 1, 0)
        owner = lax.div(place, most)
        owners.append(owner)
        lives.append(found > 0)
        starts.append(lens_ref[owner] - (place - owner * most) * page)
    wide[...] = jnp.zeros_like(wide)
    acc[...] = jnp.zeros_like(acc)
    at_request = lax.broadcasted_iota(jnp.int32, (requests, block), 0)
    token = lax.broadcasted_iota(jnp.int32, (page, block), 0)
    step_of = lax.div(lax.rem(lax.broadcasted_iota(jnp.int32, (page, block), 1), lines), group)
    ahead = token - step_of
    row = lax.broadcasted_iota(jnp.int32, (page, 1), 0)
    scale = 1.0 / math.sqrt(HD)
    top = jnp.full((requests, block), NEGATIVE, f32)
    for j in range(slots):
        owner, start, live = owners[j], starts[j], lives[j]
        for which, buffer in ((0, keys), (1, values)):
            loads[j][which].wait()

            @pl.when(jnp.logical_and(live, jnp.logical_and(start > -steps, start < page)))
            def _(which=which, buffer=buffer, owner=owner, start=start, j=j):
                value = buffer[j].astype(f32)
                for step in range(steps):
                    fresh = new_ref[which, pl.ds(step * requests + owner, 1), :]
                    value = jnp.where(row == start + step, fresh, value)
                buffer[j] = value.astype(bf16)

            stores[j][which].start()
        query = q_ref[pl.ds(pl.multiple_of(owner * block, block), block), :]
        for k in range(KV):
            wide[j % 2, k * lines : (k + 1) * lines, k * HD : (k + 1) * HD] = query[
                k * lines : (k + 1) * lines
            ]
        score = (
            lax.dot_general(
                keys[j], wide[j % 2], (((1,), (1,)), ((), ())), preferred_element_type=f32
            )
            * scale
        )
        limit = jnp.where(live, start, -2 * page * most)
        score = jnp.where(ahead <= limit, score, NEGATIVE)
        scores[j] = score
        best = jnp.max(score, axis=0, keepdims=True)
        top = jnp.where(at_request == owner, jnp.maximum(top, best), top)
    total = jnp.zeros((requests, block), f32)
    for j in range(slots):
        owner = owners[j]
        best = jnp.max(jnp.where(at_request == owner, top, NEGATIVE), axis=0, keepdims=True)
        score = scores[j]
        prob = jnp.where(score > 0.5 * NEGATIVE, jnp.exp(score - best), 0.0)
        prob = prob.astype(bf16).astype(f32)
        part = jnp.sum(prob, axis=0, keepdims=True)
        total = jnp.where(at_request == owner, total + part, total)
        probs[j] = jnp.transpose(prob).astype(bf16)
    for j in range(slots):
        for k in range(KV):
            part = jnp.dot(
                probs[j, k * lines : (k + 1) * lines, :],
                values[j, :, k * HD : (k + 1) * HD],
                preferred_element_type=f32,
            )
            place = pl.ds(pl.multiple_of(owners[j] * lines, lines), lines)
            acc[k, place, :] += part
    acc_ref[...] = acc[...].astype(bf16)
    stat_ref[...] = jnp.zeros_like(stat_ref)
    for k in range(KV):
        stat_ref[k, :requests, :lines] = top[:, k * lines : (k + 1) * lines]
        stat_ref[k, requests:, :lines] = total[:, k * lines : (k + 1) * lines]
    for store in stores:
        store[0].wait()
        store[1].wait()


def attend(table, lens, q, new, key_cache, value_cache, steps):
    slots, page, width = key_cache.shape
    requests = table.shape[0]
    lines = steps * (H // KV)
    bf16, f32 = jnp.bfloat16, jnp.float32
    vmem = pl.BlockSpec(memory_space=pltpu.VMEM)
    hbm = pl.BlockSpec(memory_space=pl.ANY)
    dma = pltpu.SemaphoreType.DMA
    return pl.pallas_call(
        functools.partial(attend_kernel, steps),
        name="attend",
        out_shape=(
            jax.ShapeDtypeStruct((KV, requests * lines, HD), bf16),
            jax.ShapeDtypeStruct((KV, 2 * requests, 128), f32),
            jax.ShapeDtypeStruct(key_cache.shape, bf16),
            jax.ShapeDtypeStruct(value_cache.shape, bf16),
        ),
        in_specs=[vmem, pl.BlockSpec(memory_space=pltpu.SMEM), vmem, vmem, hbm, hbm],
        out_specs=(vmem, vmem, hbm, hbm),
        scratch_shapes=[
            pltpu.VMEM(key_cache.shape, bf16),
            pltpu.VMEM(value_cache.shape, bf16),
            pltpu.VMEM((2, KV * lines, width), bf16),
            pltpu.VMEM((slots, page, KV * lines), f32),
            pltpu.VMEM((slots, KV * lines, page), bf16),
            pltpu.VMEM((KV, requests * lines, HD), f32),
            dma((2, slots)),
            dma((2, slots)),
        ],
        compiler_params=pltpu.CompilerParams(vmem_limit_bytes=32 * 2**20),
    )(table, lens, q, new, key_cache, value_cache)


def on_device(
    hidden_in,
    cache_lens,
    page_table,
    key_cache,
    value_cache,
    norm_attn,
    w_qkv,
    b_qkv,
    w_out,
    norm_mlp,
    w_gate,
    w_up,
    w_down,
):
    steps, requests, blocks, pieces = hidden_in.shape
    rows = steps * requests
    group = H // KV
    quarter = D // blocks
    seq = quarter // pieces
    zs = D // w_gate.shape[0]
    fast = (
        pieces % 128 == 0
        and w_qkv.shape[1] % 128 == 0
        and zs == blocks
        and zs % 2 == 0
        and rows <= 128
        and rows % 16 == 0
        and requests == 8
        and seq == KV
        and pieces == 256
    )
    lines = steps * group
    if fast:
        queries, fresh = project(
            cache_lens,
            hidden_in.reshape(rows, blocks * pieces),
            norm_attn.reshape(-1, 128),
            b_qkv.reshape(1, -1),
            w_qkv,
            zs,
            seq,
            steps,
        )
    else:
        flat = (
            lax.all_gather(hidden_in, "seq", axis=3, tiled=True).reshape(rows, D).astype(jnp.float32)
        )
        normed = (
            flat * lax.rsqrt(jnp.mean(flat * flat, axis=1, keepdims=True) + EPSILON) * norm_attn
        ).astype(jnp.bfloat16)
        columns = (
            jnp.dot(normed, w_qkv, preferred_element_type=jnp.float32) + b_qkv.astype(jnp.float32)
        ).astype(jnp.bfloat16)
        projected = lax.all_gather(columns, "seq", axis=1, tiled=True)
        position = (
            jnp.arange(steps, dtype=jnp.int32)[:, None] + cache_lens[None, :]
        ).reshape(rows)
        rotated = rotate(
            projected[:, : (H + KV) * HD].reshape(rows, H + KV, HD).astype(jnp.float32), position
        ).astype(jnp.bfloat16)
        queries = jnp.transpose(
            rotated[:, :H].reshape(steps, requests, KV, group, HD), (1, 2, 0, 3, 4)
        ).reshape(rows * H, HD)
        fresh = jnp.stack(
            [rotated[:, H:].reshape(rows, KV * HD), projected[:, (H + KV) * HD :]]
        ).astype(jnp.float32)
    weighted, stat, key_cache, value_cache = attend(
        page_table, cache_lens, queries, fresh, key_cache, value_cache, steps
    )

    if fast:
        output = tail(
            weighted,
            stat,
            hidden_in.reshape(rows, blocks * pieces),
            norm_mlp.reshape(-1, 128),
            w_out,
            jnp.swapaxes(w_gate, 0, 1),
            jnp.swapaxes(w_up, 0, 1),
            w_down,
            zs,
            seq,
        )
        return (output.reshape(hidden_in.shape), key_cache, value_cache)
    def by_head(value):
        value = jnp.moveaxis(value.reshape((KV, requests, steps, group) + value.shape[2:]), 1, 3)
        value = jnp.swapaxes(value, 1, 2)
        return value.reshape(seq, -1)

    def by_line(value):
        return by_head(value[:, :, :lines].reshape(KV, requests * lines))

    packed = jnp.concatenate(
        [
            by_head(weighted.astype(jnp.float32)),
            by_line(stat[:, :requests]),
            by_line(stat[:, requests:]),
        ],
        axis=1,
    )
    packed = lax.all_to_all(packed, "seq", split_axis=0, concat_axis=0, tiled=True)
    count = (H // seq) * rows
    part_acc = packed[:, : count * HD].reshape(seq, count, HD)
    part_top = packed[:, count * HD : count * (HD + 1)]
    part_sum = packed[:, count * (HD + 1) :]
    best = jnp.max(part_top, axis=0)
    share = jnp.exp(part_top - best[None])
    denominator = jnp.sum(share * part_sum, axis=0)
    numerator = jnp.sum(share[..., None] * part_acc, axis=0)
    heads = (numerator / denominator[:, None]).astype(jnp.bfloat16)
    heads = jnp.swapaxes(heads.reshape(H // seq, rows, HD), 0, 1).reshape(rows, -1)
    attended = lax.all_gather(heads, "seq", axis=1, tiled=True)
    branch_out = jnp.dot(
        attended, w_out.reshape(H * HD, blocks * pieces), preferred_element_type=jnp.float32
    ).reshape(rows, blocks, pieces)
    current = hidden_in.reshape(rows, blocks, pieces).astype(jnp.float32)
    middle = (current + branch_out).astype(jnp.bfloat16)
    rows_mid = lax.all_gather(middle, "seq", axis=2, tiled=True).astype(jnp.float32)
    inverse = lax.rsqrt(jnp.mean(rows_mid * rows_mid, axis=(1, 2), keepdims=True) + EPSILON)
    normed_mid = (rows_mid * inverse * norm_mlp.reshape(blocks, quarter)).astype(jnp.bfloat16)
    mine = lax.all_to_all(normed_mid, "req", split_axis=1, concat_axis=0, tiled=True).reshape(
        -1, quarter
    )
    gate_part = jnp.dot(mine, w_gate, preferred_element_type=jnp.float32).astype(jnp.bfloat16)
    up_part = jnp.dot(mine, w_up, preferred_element_type=jnp.float32).astype(jnp.bfloat16)
    gate_sum = lax.psum_scatter(gate_part, "req", scatter_dimension=0, tiled=True)
    up_sum = lax.psum_scatter(up_part, "req", scatter_dimension=0, tiled=True)
    hidden_part = (
        jax.nn.silu(gate_sum.astype(jnp.float32)) * up_sum.astype(jnp.float32)
    ).astype(jnp.bfloat16)
    hidden = lax.all_gather(hidden_part, "req", axis=0, tiled=True)
    down = jnp.dot(hidden, w_down, preferred_element_type=jnp.float32)
    sums = lax.psum_scatter(
        down.reshape(down.shape[0], 1, quarter).astype(jnp.bfloat16),
        "seq",
        scatter_dimension=2,
        tiled=True,
    ).astype(jnp.float32)
    back = lax.all_to_all(sums, "req", split_axis=0, concat_axis=1, tiled=True)
    output = (middle.astype(jnp.float32) + back).astype(jnp.bfloat16)
    return (output.reshape(hidden_in.shape), key_cache, value_cache)


def solution(mesh):
    in_specs = (
        P(None, "req", None, "seq"),
        P("req"),
        P("req", None),
        P(("req", "seq"), None, None),
        P(("req", "seq"), None, None),
        P(),
        P(None, "seq"),
        P("seq"),
        P(None, None, "seq"),
        P(),
        P("req", "seq"),
        P("req", "seq"),
        P("seq", "req"),
    )
    out_specs = (
        P(None, "req", None, "seq"),
        P(("req", "seq"), None, None),
        P(("req", "seq"), None, None),
    )
    return jax.shard_map(
        on_device, mesh=mesh, in_specs=in_specs, out_specs=out_specs, check_vma=False
    )
```

```python
import functools
import math

import jax
import jax.numpy as jnp
from jax import lax
from jax.experimental import pallas as pl
from jax.experimental.pallas import tpu as pltpu
from jax.sharding import PartitionSpec as P

D = 8192
H = 64
KV = 8
HD = 128
STEPS = 4


EPSILON = 1e-06
THETA = 1000000.0
NEGATIVE = -1e30


def rotate(heads, position):
    half = heads.shape[-1] // 2
    freq = THETA ** (-(jnp.arange(half, dtype=jnp.float32) * 2.0 / heads.shape[-1]))
    angle = position.astype(jnp.float32)[:, None, None] * freq[None, None, :]
    cosine = jnp.cos(angle)
    sine = jnp.sin(angle)
    first = heads[..., :half]
    second = heads[..., half:]
    return jnp.concatenate(
        [first * cosine - second * sine, second * cosine + first * sine], axis=-1
    )


MESH = pl.DeviceIdType.MESH


def greet(partners):
    barrier = pltpu.get_barrier_semaphore()
    for partner in partners:
        pl.semaphore_signal(barrier, inc=1, device_id=partner, device_id_type=MESH)
    pl.semaphore_wait(barrier, len(partners))


def remote(src, dst, send, recv, partner):
    return pltpu.make_async_remote_copy(
        src_ref=src,
        dst_ref=dst,
        send_sem=send,
        recv_sem=recv,
        device_id=partner,
        device_id_type=MESH,
    )


class Gather:
    def __init__(self, z, s, ss, dst, send, recv):
        def flip(value, bit):
            return value + bit - 2 * bit * lax.rem(lax.div(value, bit), 2)

        self.twin = flip(s, 1)
        self.peers = []
        for mask in range(1, ss // 2):
            value, bit = s, 2
            while bit < ss:
                if mask & (bit // 2):
                    value = flip(value, bit)
                bit *= 2
            self.peers.append(value)
        count = len(self.peers)
        self.slots = (
            [s, self.twin] + self.peers + [flip(peer, 1) for peer in self.peers]
        )
        twin = {"req": z, "seq": self.twin}
        self.partners = [twin] + [{"req": z, "seq": peer} for peer in self.peers]
        self.parts = list(zip(dst, send, recv))
        self.direct, self.onward = [], []
        for i, partner in enumerate(self.partners):
            self.direct.append(
                [remote(d.at[s], d.at[s], a.at[i], b.at[i], partner) for d, a, b in self.parts]
            )
        for i, peer in enumerate(self.peers):
            at = count + 1 + i
            self.onward.append(
                [remote(d.at[peer], d.at[peer], a.at[at], b.at[at], twin) for d, a, b in self.parts]
            )

    def start(self):
        for copies in self.direct:
            for copy in copies:
                copy.start()

    def wait(self, step):
        if step == 0:
            return
        if step <= len(self.direct):
            for copy in self.direct[step - 1]:
                copy.wait_recv()
            if step > 1:
                for copy in self.onward[step - 2]:
                    copy.start()
        else:
            for copy in self.onward[step - 1 - len(self.direct)]:
                copy.wait_recv()

    def wait_all(self):
        for step in range(len(self.slots)):
            self.wait(step)

    def wait_sent(self):
        for copies in self.direct + self.onward:
            for copy in copies:
                copy.wait_send()


WIDTH = 128
PANEL = 256
LAGS = (0, 10, 14, 33, 38, 46, 56)
RING = 6
KEPT = 4
EARLY = 5
NEXT = 10


def tail_kernel(
    zs,
    ss,
    width,
    acc_ref,
    stat_ref,
    x_ref,
    norm_hbm,
    wo_hbm,
    wg_hbm,
    wu_hbm,
    wd_hbm,
    out_ref,
    wo,
    wg,
    wu,
    wd,
    got_acc,
    got_stat,
    mixed,
    everyone,
    pick,
    lay,
    mid,
    cut,
    square,
    gains,
    got,
    got_sq,
    normed,
    own_g,
    own_u,
    send_r,
    recv_r,
    send_l,
    recv_l,
    hid,
    down,
    parts,
    landed,
    sums,
    back,
    wo_sem,
    w_sem,
    wd_sem,
    in_sem,
    m_send,
    m_recv,
    h_send,
    h_recv,
    a_send,
    a_recv,
    b_send,
    b_recv,
    rs_send,
    rs_recv,
    ag_send,
    ag_recv,
    d_send,
    d_recv,
    e_send,
    e_recv,
):
    z = lax.axis_index("req")
    s = lax.axis_index("seq")
    f32, bf16 = jnp.float32, jnp.bfloat16
    rows, features = mid.shape
    pieces = features // zs
    stride = x_ref.shape[0] // rows
    per = H // ss
    units = wg.shape[0]
    half = zs * rows // 2
    starts = list(range(0, units, width))
    count = len(starts)
    sizes = [min(width, units - start) for start in starts]
    padded = [-(-size // 128) * 128 for size in sizes]
    ratio = PANEL // width
    tops = list(range(0, units, PANEL))
    panels = len(tops)
    heights = [min(PANEL, units - top) for top in tops]
    z_partners = [{"req": lax.rem(z + k, zs), "seq": s} for k in range(1, zs)]
    s_partners = [{"req": z, "seq": lax.rem(s + k, ss)} for k in range(1, ss)]
    attended = Gather(z, s, ss, [everyone], [h_send], [h_recv])
    depth = D // ss

    def wo_load(n):
        first_row = pl.multiple_of(attended.slots[n] * depth, depth)
        return pltpu.make_async_copy(
            wo_hbm.at[pl.ds(first_row, depth)], wo.at[n % KEPT], wo_sem.at[n % KEPT]
        )

    def wd_load(m):
        return pltpu.make_async_copy(
            wd_hbm.at[pl.ds(tops[m], heights[m])],
            wd.at[m % RING, pl.ds(0, heights[m])],
            wd_sem.at[m % RING],
        )

    def panel_loads(m):
        lines = pl.ds(tops[m], heights[m])
        return (
            pltpu.make_async_copy(wg_hbm.at[lines], wg.at[lines], w_sem.at[0, m]),
            pltpu.make_async_copy(wu_hbm.at[lines], wu.at[lines], w_sem.at[1, m]),
        )

    def start_panels(low, high):
        for m in range(min(low, panels), min(high, panels)):
            for load in panel_loads(m):
                load.start()

    staged = [
        pltpu.make_async_copy(acc_ref.at[s], got_acc.at[s], in_sem.at[0]),
        pltpu.make_async_copy(stat_ref.at[s], got_stat.at[s], in_sem.at[1]),
        pltpu.make_async_copy(norm_hbm, gains, in_sem.at[2]),
    ]
    for load in staged:
        load.start()
    for n in range(KEPT):
        wo_load(n).start()
    start_panels(0, EARLY)
    greet(z_partners + s_partners)

    first = []
    for k in range(1, ss):
        to = lax.rem(s + k, ss)
        first.append(
            remote(stat_ref.at[to], got_stat.at[s], m_send.at[1, k], m_recv.at[1, k], s_partners[k - 1])
        )
        first.append(
            remote(acc_ref.at[to], got_acc.at[s], m_send.at[0, k], m_recv.at[0, k], s_partners[k - 1])
        )
    for copy in first:
        copy.start()
    lay[...] = x_ref[...].astype(f32)
    span = zs * 256
    pick[...] = jnp.where(
        lax.div(lax.broadcasted_iota(jnp.int32, (256, span), 1), zs)
        == lax.broadcasted_iota(jnp.int32, (256, span), 0),
        1.0,
        0.0,
    ).astype(bf16)
    for load in staged:
        load.wait()
    for copy in first:
        copy.wait_recv()
    start_panels(EARLY, NEXT)
    requests = stat_ref.shape[1] // 2
    lines = rows // requests * per
    best = got_stat[0, :requests]
    for other in range(1, ss):
        best = jnp.maximum(best, got_stat[other, :requests])
    shares = [jnp.exp(got_stat[other, :requests] - best) for other in range(ss)]
    denominator = shares[0] * got_stat[0, requests:]
    for other in range(1, ss):
        denominator = denominator + shares[other] * got_stat[other, requests:]
    lane = lax.broadcasted_iota(jnp.int32, denominator.shape, 1)
    denominator = jnp.where(lane < lines, denominator, 1.0)
    tall = jnp.transpose(jnp.concatenate([share / denominator for share in shares], axis=0))
    for request in range(requests):
        place = slice(request * lines, (request + 1) * lines)
        value = got_acc[0, place, :].astype(f32) * tall[:lines, request : request + 1]
        for other in range(1, ss):
            at = other * requests + request
            value = value + got_acc[other, place, :].astype(f32) * tall[:lines, at : at + 1]
        mixed[place, :] = value
    for head in range(per):
        column = [
            mixed[pl.ds(step * per + head, requests, stride=lines), :]
            for step in range(rows // requests)
        ]
        everyone[s, :, head * HD : (head + 1) * HD] = jnp.concatenate(column, axis=0).astype(bf16)
    attended.start()

    which = lax.rem(lax.broadcasted_iota(jnp.int32, (rows, span), 1), zs)
    result = jnp.zeros((zs * rows, pieces), f32)
    for n in range(ss):
        attended.wait(n)
        block = everyone[attended.slots[n]]
        chunks = depth // 256
        tower = jnp.concatenate([block[:, c * 256 : (c + 1) * 256] for c in range(chunks)], axis=0)
        spread = jnp.dot(tower, pick[...], preferred_element_type=f32)
        wo_load(n).wait()
        for c in range(chunks):
            line = spread[c * rows : (c + 1) * rows]
            left = jnp.concatenate(
                [jnp.where(which == b, line, 0.0) for b in range(zs)], axis=0
            ).astype(bf16)
            right = wo[n % KEPT, c * 256 : (c + 1) * 256].reshape(span, pieces)
            result = result + jnp.dot(left, right, preferred_element_type=f32)
        if n + KEPT < ss:
            wo_load(n + KEPT).start()
    start_panels(NEXT, panels)
    for m in range(min(RING, panels)):
        wd_load(m).start()
    total = jnp.zeros((8, rows), f32)
    for block in range(zs):
        cols = slice(block * pieces, (block + 1) * pieces)
        came_in = jnp.concatenate(
            [
                lay[pl.ds(part * zs + block, rows, stride=stride), :]
                for part in range(pieces // 128)
            ],
            axis=1,
        )
        piece = (came_in + result[block * rows : (block + 1) * rows]).astype(bf16)
        mid[:, cols] = piece
        cut[block] = piece
        value = piece.astype(f32)
        total += lax.dot_general(
            jnp.ones((8, pieces), f32),
            value * value,
            (((1,), (1,)), ((), ())),
            precision=lax.Precision.HIGHEST,
            preferred_element_type=f32,
        )
    square[...] = jnp.zeros_like(square)
    square[:, :rows] = total
    second = []
    for k in range(1, zs):
        to = lax.rem(z + k, zs)
        second.append(
            remote(cut.at[to], got.at[s, z], a_send.at[0, k], a_recv.at[0, k], z_partners[k - 1])
        )
        second.append(
            remote(square, got_sq.at[s, z], a_send.at[1, k], a_recv.at[1, k], z_partners[k - 1])
        )
    for copy in second:
        copy.start()
    got[s, z] = cut[z]
    got_sq[s, z] = square[...]
    for copy in second:
        copy.wait_recv()
    blocks = Gather(z, s, ss, [got, got_sq], [b_send.at[0], b_send.at[1]], [b_recv.at[0], b_recv.at[1]])
    blocks.start()
    if sizes[-1] != padded[-1]:
        send_r[count - 1] = jnp.zeros_like(send_r[count - 1])
        send_l[count - 1] = jnp.zeros_like(send_l[count - 1])
        hid[panels - 1] = jnp.zeros_like(hid[panels - 1])
    down[...] = jnp.zeros_like(down)
    blocks.wait_all()
    for group in range(zs):
        line = got_sq[0, group]
        for other in range(1, ss):
            line = line + got_sq[other, group]
        spread = lax.dot_general(
            line[:, :rows],
            jnp.full((8, 128), 0.125, f32),
            (((0,), (0,)), ((), ())),
            precision=lax.Precision.HIGHEST,
            preferred_element_type=f32,
        )
        inverse = lax.rsqrt(spread / D + EPSILON)
        for other in range(ss):
            for part in range(pieces // 128):
                at = other * pieces + part * 128
                gain = gains[pl.ds(z * (ss * pieces // 128) + at // 128, 1), :]
                value = got[other, group, :, part * 128 : (part + 1) * 128].astype(f32)
                normed[group * rows : (group + 1) * rows, at : at + 128] = (
                    value * inverse * gain
                ).astype(bf16)

    right = {"req": lax.rem(z + 1, zs), "seq": s}
    left = {"req": lax.rem(z + zs - 1, zs), "seq": s}

    def reduce_copy(way, p):
        src, dst, to = ((send_r, recv_r, right), (send_l, recv_l, left))[way]
        lanes = pl.ds(0, 2 * padded[p])
        return remote(
            src.at[p, :, lanes], dst.at[p, :, lanes], rs_send.at[way, p], rs_recv.at[way, p], to
        )

    def hidden_copy(way, p):
        place = (
            p // ratio,
            pl.ds(half * (1 - way), half),
            pl.ds(p % ratio * width, padded[p]),
        )
        return remote(
            hid.at[place],
            hid.at[place],
            ag_send.at[way, p],
            ag_recv.at[way, p],
            (left, right)[way],
        )

    def reduce_step(way, p, place):
        size, pad = sizes[p], padded[p]
        base = half * (1 - way)
        cols = slice(starts[p], starts[p] + size)
        gate = own_g[base : base + half, cols]
        up = own_u[base : base + half, cols]
        if place > 0:
            reduce_copy(way, p).wait_recv()
            came = (recv_r, recv_l)[way]
            gate = gate + came[p, :, :size].astype(f32)
            up = up + came[p, :, pad : pad + size].astype(f32)
        if place < zs - 1:
            goes = (send_r, send_l)[way]
            goes[p, :, :size] = gate.astype(bf16)
            goes[p, :, pad : pad + size] = up.astype(bf16)
            reduce_copy(way, p).start()
        else:
            gate = gate.astype(bf16).astype(f32)
            up = up.astype(bf16).astype(f32)
            low = p % ratio * width
            hid[p // ratio, base : base + half, low : low + size] = (
                gate / (1.0 + jnp.exp(-gate)) * up
            ).astype(bf16)
            hidden_copy(way, p).start()

    def down_step(m):
        wd_load(m).wait()
        down[...] += jnp.dot(
            hid[m, :, : heights[m]], wd[m % RING, : heights[m], :], preferred_element_type=f32
        )
        if m + RING < panels:
            wd_load(m + RING).start()

    nt = (((1,), (1,)), ((), ()))
    lag = LAGS if zs == 4 else tuple(2 * i for i in range(2 * zs - 1))
    last = lag[2 * zs - 2]
    for i in range(count + last):
        if i < count and i % ratio == 0:
            m = i // ratio
            cols = slice(tops[m], tops[m] + heights[m])
            for load in panel_loads(m):
                load.wait()
            own_g[:, cols] = lax.dot_general(normed[...], wg[cols, :], nt, preferred_element_type=f32)
            own_u[:, cols] = lax.dot_general(normed[...], wu[cols, :], nt, preferred_element_type=f32)
        for zz in range(zs):

            @pl.when(z == zz)
            def _(zz=zz, i=i):
                order = (0, 1) if zz < zs // 2 else (1, 0)
                for way in order:
                    place = zz if way == 0 else zs - 1 - zz
                    p = i - lag[place]
                    if 0 <= p < count:
                        reduce_step(way, p, place)
                for way in order[::-1]:
                    place = zs - 1 - zz if way == 0 else zz
                    p = i - lag[zs - 1 + place]
                    if place > 0 and 0 <= p < count:
                        hidden_copy(way, p).wait_recv()
                        if place < zs - 1:
                            hidden_copy(way, p).start()

        p = i - last
        if p >= 0 and (p % ratio == ratio - 1 or p == count - 1):
            down_step(p // ratio)

    for other in range(ss):
        parts[other] = down[:, other * pieces : (other + 1) * pieces].astype(bf16)
    third = []
    for k in range(1, ss):
        to = lax.rem(s + k, ss)
        third.append(
            remote(parts.at[to], landed.at[s], d_send.at[k], d_recv.at[k], s_partners[k - 1])
        )
    for copy in third:
        copy.start()
    landed[s] = parts[s]
    for copy in third:
        copy.wait_recv()
    whole = landed[0].astype(f32)
    for other in range(1, ss):
        whole = whole + landed[other].astype(f32)
    for group in range(zs):
        sums[group] = whole[group * rows : (group + 1) * rows]
    fourth = []
    for k in range(1, zs):
        to = lax.rem(z + k, zs)
        fourth.append(
            remote(sums.at[to], back.at[z], e_send.at[k], e_recv.at[k], z_partners[k - 1])
        )
    for copy in fourth:
        copy.start()
    back[z] = sums[z]
    for copy in fourth:
        copy.wait_recv()
    for block in range(zs):
        cols = slice(block * pieces, (block + 1) * pieces)
        value = mid[:, cols].astype(f32) + back[block]
        for part in range(pieces // 128):
            lay[pl.ds(part * zs + block, rows, stride=stride), :] = value[
                :, part * 128 : (part + 1) * 128
            ]
    out_ref[...] = lay[...].astype(bf16)

    for copy in first + second + third + fourth:
        copy.wait_send()
    attended.wait_sent()
    blocks.wait_sent()
    for way in range(2):
        for p in range(count):

            @pl.when(z != (zs - 1 if way == 0 else 0))
            def _(way=way, p=p):
                reduce_copy(way, p).wait_send()

            @pl.when(z != (0 if way == 0 else zs - 1))
            def _(way=way, p=p):
                hidden_copy(way, p).wait_send()


def tail(acc, stat, x, norm, w_out, w_gate, w_up, w_down, zs, ss):
    features = w_out.shape[1] * w_out.shape[2]
    rows = x.shape[0] * 128 // features
    pieces = features // zs
    units, depth = w_gate.shape
    quarter = w_down.shape[1]
    width = WIDTH
    count = -(-units // width)
    panels = -(-units // PANEL)
    everyone = zs * rows
    half = everyone // 2
    bf16, f32 = jnp.bfloat16, jnp.float32
    vmem = pl.BlockSpec(memory_space=pltpu.VMEM)
    hbm = pl.BlockSpec(memory_space=pl.ANY)
    dma = pltpu.SemaphoreType.DMA
    return pl.pallas_call(
        functools.partial(tail_kernel, zs, ss, width),
        name="tail",
        out_shape=jax.ShapeDtypeStruct(x.shape, bf16),
        in_specs=[hbm, hbm, vmem, hbm, hbm, hbm, hbm, hbm],
        out_specs=vmem,
        scratch_shapes=[
            pltpu.VMEM((KEPT, D // ss) + w_out.shape[1:], bf16),
            pltpu.VMEM(w_gate.shape, bf16),
            pltpu.VMEM(w_up.shape, bf16),
            pltpu.VMEM((RING, PANEL, quarter), bf16),
            pltpu.VMEM(acc.shape, bf16),
            pltpu.VMEM(stat.shape, f32),
            pltpu.VMEM(acc.shape[1:], f32),
            pltpu.VMEM((ss, rows, H // ss * HD), bf16),
            pltpu.VMEM((256, zs * 256), bf16),
            pltpu.VMEM(x.shape, f32),
            pltpu.VMEM((rows, features), bf16),
            pltpu.VMEM((zs, rows, pieces), bf16),
            pltpu.VMEM((8, 128), f32),
            pltpu.VMEM(norm.shape, f32),
            pltpu.VMEM((ss, zs, rows, pieces), bf16),
            pltpu.VMEM((ss, zs, 8, 128), f32),
            pltpu.VMEM((everyone, depth), bf16),
            pltpu.VMEM((everyone, units), f32),
            pltpu.VMEM((everyone, units), f32),
            pltpu.VMEM((count, half, 2 * width), bf16),
            pltpu.VMEM((count, half, 2 * width), bf16),
            pltpu.VMEM((count, half, 2 * width), bf16),
            pltpu.VMEM((count, half, 2 * width), bf16),
            pltpu.VMEM((panels, everyone, PANEL), bf16),
            pltpu.VMEM((everyone, quarter), f32),
            pltpu.VMEM((ss, everyone, pieces), bf16),
            pltpu.VMEM((ss, everyone, pieces), bf16),
            pltpu.VMEM((zs, rows, pieces), f32),
            pltpu.VMEM((zs, rows, pieces), f32),
            dma((KEPT,)),
            dma((2, panels)),
            dma((RING,)),
            dma((3,)),
            dma((2, ss)),
            dma((2, ss)),
            dma((ss,)),
            dma((ss,)),
            dma((2, zs)),
            dma((2, zs)),
            dma((2, ss)),
            dma((2, ss)),
            dma((2, count)),
            dma((2, count)),
            dma((2, count)),
            dma((2, count)),
            dma((ss,)),
            dma((ss,)),
            dma((zs,)),
            dma((zs,)),
        ],
        compiler_params=pltpu.CompilerParams(
            collective_id=0, has_side_effects=True, vmem_limit_bytes=61 * 2**20
        ),
    )(acc, stat, x, norm, w_out, w_gate, w_up, w_down)


def project_kernel(
    zs,
    ss,
    steps,
    x_ref,
    fixed_ref,
    w_hbm,
    q_ref,
    new_ref,
    w,
    lay,
    got,
    normed,
    columns_a,
    columns_b,
    spread,
    w_sem,
    a_send,
    a_recv,
    b_send,
    b_recv,
):
    z = lax.axis_index("req")
    s = lax.axis_index("seq")
    f32 = jnp.float32
    rows, features = got.shape[1:]
    requests = rows // steps
    blocks = zs
    pieces = features // blocks
    stride = x_ref.shape[0] // rows
    mine = w.shape[1]
    local = mine // HD
    group = H // KV
    parts = 4
    depth = D // parts
    cuts = [0, columns_a.shape[2], mine]
    halves = (columns_a, columns_b)

    def load(which, part):
        place = (pl.ds(part * depth, depth), pl.ds(cuts[which], cuts[which + 1] - cuts[which]))
        return pltpu.make_async_copy(w_hbm.at[place], w.at[place], w_sem.at[which, part])

    inputs = Gather(z, s, ss, [got], [a_send], [a_recv])
    outputs = [
        Gather(z, s, ss, [halves[i]], [b_send.at[i]], [b_recv.at[i]]) for i in range(2)
    ]
    for which in range(2):
        for part in range(parts):
            load(which, part).start()
    lay[...] = x_ref[...].astype(f32)
    for block in range(blocks):
        for part in range(pieces // 128):
            at = block * pieces + part * 128
            got[s, :, at : at + 128] = lay[
                pl.ds(part * blocks + block, rows, stride=stride), :
            ].astype(jnp.bfloat16)
    greet(inputs.partners)
    inputs.start()
    row = lax.broadcasted_iota(jnp.int32, (rows, HD), 0)
    lane = lax.broadcasted_iota(jnp.int32, (rows, HD), 1)
    lens = fixed_ref[(D + mine) // 128 : (D + mine) // 128 + 1, :]
    position = lax.div(row, requests).astype(f32) + jnp.sum(
        jnp.where(lane == lax.rem(row, requests), lens, 0.0), axis=1, keepdims=True
    )
    entry = lax.rem(lane, HD // 2).astype(f32)
    angle = position * jnp.exp(entry * (-2.0 * math.log(THETA) / HD))
    cosine = jnp.cos(angle)
    sine = jnp.where(lane < HD // 2, -jnp.sin(angle), jnp.sin(angle))
    inputs.wait_all()
    total = jnp.zeros((rows, 1), f32)
    for other in range(ss):
        value = got[other].astype(f32)
        total += jnp.sum(value * value, axis=1, keepdims=True)
    inverse = lax.rsqrt(total / D + EPSILON)
    for other in range(ss):
        for block in range(blocks):
            base = block * ss * pieces + other * pieces
            for line in range(pieces // 128):
                at = base + line * 128
                value = got[
                    other, :, block * pieces + line * 128 : block * pieces + (line + 1) * 128
                ].astype(f32)
                gain = fixed_ref[at // 128 : at // 128 + 1, :]
                normed[:, at : at + 128] = (value * inverse * gain).astype(jnp.bfloat16)
    bias = fixed_ref[D // 128 : (D + mine) // 128, :]
    for which in range(2):
        low, high = cuts[which], cuts[which + 1]
        result = jnp.zeros((rows, high - low), f32)
        for part in range(parts):
            load(which, part).wait()
            span = slice(part * depth, (part + 1) * depth)
            result += jnp.dot(normed[:, span], w[span, low:high], preferred_element_type=f32)
        for head in range(low // HD, high // HD):
            at = head * HD - low
            tile = (result[:, at : at + HD] + bias[head : head + 1]).astype(jnp.bfloat16).astype(f32)
            turned = tile * cosine + pltpu.roll(tile, HD // 2, axis=1) * sine
            halves[which][s, :, at : at + HD] = jnp.where(
                s * local + head < H + KV, turned, tile
            ).astype(jnp.bfloat16)
        outputs[which].start()
    for which in range(2):
        low, high = cuts[which], cuts[which + 1]
        outputs[which].wait_all()
        for head in range(H + 2 * KV):
            other, at = head // local, (head % local) * HD
            if not low <= at < high:
                continue
            tile = halves[which][other, :, at - low : at - low + HD].astype(f32)
            if head < H:
                for step in range(steps):
                    base = (head // group) * steps * group + step * group + head % group
                    spread[pl.ds(base, requests, stride=H * steps), :] = tile[
                        step * requests : (step + 1) * requests
                    ]
            else:
                at = ((head - H) % KV) * HD
                new_ref[(head - H) // KV, :, at : at + HD] = tile
    q_ref[...] = spread[...].astype(jnp.bfloat16)
    inputs.wait_sent()
    for output in outputs:
        output.wait_sent()


def project(lens, x, norm, bias, w, zs, ss, steps):
    features = D // ss
    rows = x.shape[0] * 128 // features
    mine = w.shape[1]
    fixed = jnp.concatenate(
        [
            norm,
            bias.astype(jnp.float32),
            lens.astype(jnp.float32),
            jnp.zeros(128 - lens.shape[0], jnp.float32),
        ]
    ).reshape(-1, 128)
    first = mine // HD * 3 // 5 * HD
    bf16, f32 = jnp.bfloat16, jnp.float32
    vmem = pl.BlockSpec(memory_space=pltpu.VMEM)
    dma = pltpu.SemaphoreType.DMA
    return pl.pallas_call(
        functools.partial(project_kernel, zs, ss, steps),
        name="project",
        out_shape=(
            jax.ShapeDtypeStruct((rows * H, HD), bf16),
            jax.ShapeDtypeStruct((2, rows, KV * HD), f32),
        ),
        in_specs=[
            vmem,
            vmem,
            pl.BlockSpec(memory_space=pl.ANY),
        ],
        out_specs=(vmem, vmem),
        scratch_shapes=[
            pltpu.VMEM(w.shape, bf16),
            pltpu.VMEM(x.shape, f32),
            pltpu.VMEM((ss, rows, features), bf16),
            pltpu.VMEM((rows, D), bf16),
            pltpu.VMEM((ss, rows, first), bf16),
            pltpu.VMEM((ss, rows, mine - first), bf16),
            pltpu.VMEM((rows * H, HD), f32),
            dma((2, 4)),
            dma((ss,)),
            dma((ss,)),
            dma((2, ss)),
            dma((2, ss)),
        ],
        compiler_params=pltpu.CompilerParams(
            collective_id=1, has_side_effects=True, vmem_limit_bytes=48 * 2**20
        ),
    )(x, fixed, w)


def attend_kernel(
    steps,
    table_ref,
    lens_ref,
    q_ref,
    new_ref,
    k_hbm,
    v_hbm,
    acc_ref,
    stat_ref,
    ko_hbm,
    vo_hbm,
    keys,
    values,
    wide,
    scores,
    probs,
    acc,
    in_sem,
    out_sem,
):
    f32, bf16 = jnp.float32, jnp.bfloat16
    slots, page, _ = keys.shape
    requests, most = table_ref.shape
    group = H // KV
    lines = steps * group
    block = KV * lines
    loads = [
        (
            pltpu.make_async_copy(k_hbm.at[j], keys.at[j], in_sem.at[0, j]),
            pltpu.make_async_copy(v_hbm.at[j], values.at[j], in_sem.at[1, j]),
        )
        for j in range(slots)
    ]
    for load in loads:
        load[0].start()
    for load in loads:
        load[1].start()
    stores = [
        (
            pltpu.make_async_copy(keys.at[j], ko_hbm.at[j], out_sem.at[0, j]),
            pltpu.make_async_copy(values.at[j], vo_hbm.at[j], out_sem.at[1, j]),
        )
        for j in range(slots)
    ]
    base = lax.axis_index("seq") * slots
    table = table_ref[...]
    code = (
        lax.broadcasted_iota(jnp.int32, table.shape, 0) * most
        + lax.broadcasted_iota(jnp.int32, table.shape, 1)
        + 1
    ).astype(f32)
    owners, starts, lives = [], [], []
    for j in range(slots):
        found = jnp.max(jnp.where(table == base + j, code, 0.0)).astype(jnp.int32)
        place = jnp.maximum(found - 1, 0)
        owner = lax.div(place, most)
        owners.append(owner)
        lives.append(found > 0)
        starts.append(lens_ref[owner] - (place - owner * most) * page)
    wide[...] = jnp.zeros_like(wide)
    acc[...] = jnp.zeros_like(acc)
    at_request = lax.broadcasted_iota(jnp.int32, (requests, block), 0)
    token = lax.broadcasted_iota(jnp.int32, (page, block), 0)
    step_of = lax.div(lax.rem(lax.broadcasted_iota(jnp.int32, (page, block), 1), lines), group)
    ahead = token - step_of
    row = lax.broadcasted_iota(jnp.int32, (page, 1), 0)
    scale = 1.0 / math.sqrt(HD)
    top = jnp.full((requests, block), NEGATIVE, f32)
    for j in range(slots):
        owner, start, live = owners[j], starts[j], lives[j]
        for which, buffer in ((0, keys), (1, values)):
            loads[j][which].wait()

            @pl.when(jnp.logical_and(live, jnp.logical_and(start > -steps, start < page)))
            def _(which=which, buffer=buffer, owner=owner, start=start, j=j):
                value = buffer[j].astype(f32)
                for step in range(steps):
                    fresh = new_ref[which, pl.ds(step * requests + owner, 1), :]
                    value = jnp.where(row == start + step, fresh, value)
                buffer[j] = value.astype(bf16)

            stores[j][which].start()
        query = q_ref[pl.ds(pl.multiple_of(owner * block, block), block), :]
        for k in range(KV):
            wide[j % 2, k * lines : (k + 1) * lines, k * HD : (k + 1) * HD] = query[
                k * lines : (k + 1) * lines
            ]
        score = (
            lax.dot_general(
                keys[j], wide[j % 2], (((1,), (1,)), ((), ())), preferred_element_type=f32
            )
            * scale
        )
        limit = jnp.where(live, start, -2 * page * most)
        score = jnp.where(ahead <= limit, score, NEGATIVE)
        scores[j] = score
        best = jnp.max(score, axis=0, keepdims=True)
        top = jnp.where(at_request == owner, jnp.maximum(top, best), top)
    total = jnp.zeros((requests, block), f32)
    for j in range(slots):
        owner = owners[j]
        best = jnp.max(jnp.where(at_request == owner, top, NEGATIVE), axis=0, keepdims=True)
        score = scores[j]
        prob = jnp.where(score > 0.5 * NEGATIVE, jnp.exp(score - best), 0.0)
        prob = prob.astype(bf16).astype(f32)
        part = jnp.sum(prob, axis=0, keepdims=True)
        total = jnp.where(at_request == owner, total + part, total)
        probs[j] = jnp.transpose(prob).astype(bf16)
    for j in range(slots):
        for k in range(KV):
            part = jnp.dot(
                probs[j, k * lines : (k + 1) * lines, :],
                values[j, :, k * HD : (k + 1) * HD],
                preferred_element_type=f32,
            )
            place = pl.ds(pl.multiple_of(owners[j] * lines, lines), lines)
            acc[k, place, :] += part
    acc_ref[...] = acc[...].astype(bf16)
    stat_ref[...] = jnp.zeros_like(stat_ref)
    for k in range(KV):
        stat_ref[k, :requests, :lines] = top[:, k * lines : (k + 1) * lines]
        stat_ref[k, requests:, :lines] = total[:, k * lines : (k + 1) * lines]
    for store in stores:
        store[0].wait()
        store[1].wait()


def attend(table, lens, q, new, key_cache, value_cache, steps):
    slots, page, width = key_cache.shape
    requests = table.shape[0]
    lines = steps * (H // KV)
    bf16, f32 = jnp.bfloat16, jnp.float32
    vmem = pl.BlockSpec(memory_space=pltpu.VMEM)
    hbm = pl.BlockSpec(memory_space=pl.ANY)
    dma = pltpu.SemaphoreType.DMA
    return pl.pallas_call(
        functools.partial(attend_kernel, steps),
        name="attend",
        out_shape=(
            jax.ShapeDtypeStruct((KV, requests * lines, HD), bf16),
            jax.ShapeDtypeStruct((KV, 2 * requests, 128), f32),
            jax.ShapeDtypeStruct(key_cache.shape, bf16),
            jax.ShapeDtypeStruct(value_cache.shape, bf16),
        ),
        in_specs=[vmem, pl.BlockSpec(memory_space=pltpu.SMEM), vmem, vmem, hbm, hbm],
        out_specs=(vmem, vmem, hbm, hbm),
        scratch_shapes=[
            pltpu.VMEM(key_cache.shape, bf16),
            pltpu.VMEM(value_cache.shape, bf16),
            pltpu.VMEM((2, KV * lines, width), bf16),
            pltpu.VMEM((slots, page, KV * lines), f32),
            pltpu.VMEM((slots, KV * lines, page), bf16),
            pltpu.VMEM((KV, requests * lines, HD), f32),
            dma((2, slots)),
            dma((2, slots)),
        ],
        compiler_params=pltpu.CompilerParams(vmem_limit_bytes=32 * 2**20),
    )(table, lens, q, new, key_cache, value_cache)


def on_device(
    hidden_in,
    cache_lens,
    page_table,
    key_cache,
    value_cache,
    norm_attn,
    w_qkv,
    b_qkv,
    w_out,
    norm_mlp,
    w_gate,
    w_up,
    w_down,
):
    steps, requests, blocks, pieces = hidden_in.shape
    rows = steps * requests
    group = H // KV
    quarter = D // blocks
    seq = quarter // pieces
    zs = D // w_gate.shape[0]
    fast = (
        pieces % 128 == 0
        and w_qkv.shape[1] % 128 == 0
        and zs == blocks
        and zs % 2 == 0
        and rows <= 128
        and rows % 16 == 0
        and requests == 8
        and seq == KV
        and pieces == 256
    )
    lines = steps * group
    if fast:
        lying = jnp.swapaxes(
            hidden_in.reshape(steps, requests, blocks, pieces // 128, 128), 2, 3
        ).reshape(-1, 128)
        queries, fresh = project(
            cache_lens,
            lying,
            norm_attn,
            b_qkv,
            w_qkv,
            zs,
            seq,
            steps,
        )
    else:
        flat = (
            lax.all_gather(hidden_in, "seq", axis=3, tiled=True).reshape(rows, D).astype(jnp.float32)
        )
        normed = (
            flat * lax.rsqrt(jnp.mean(flat * flat, axis=1, keepdims=True) + EPSILON) * norm_attn
        ).astype(jnp.bfloat16)
        columns = (
            jnp.dot(normed, w_qkv, preferred_element_type=jnp.float32) + b_qkv.astype(jnp.float32)
        ).astype(jnp.bfloat16)
        projected = lax.all_gather(columns, "seq", axis=1, tiled=True)
        position = (
            jnp.arange(steps, dtype=jnp.int32)[:, None] + cache_lens[None, :]
        ).reshape(rows)
        rotated = rotate(
            projected[:, : (H + KV) * HD].reshape(rows, H + KV, HD).astype(jnp.float32), position
        ).astype(jnp.bfloat16)
        queries = jnp.transpose(
            rotated[:, :H].reshape(steps, requests, KV, group, HD), (1, 2, 0, 3, 4)
        ).reshape(rows * H, HD)
        fresh = jnp.stack(
            [rotated[:, H:].reshape(rows, KV * HD), projected[:, (H + KV) * HD :]]
        ).astype(jnp.float32)
    weighted, stat, key_cache, value_cache = attend(
        page_table, cache_lens, queries, fresh, key_cache, value_cache, steps
    )

    if fast:
        output = tail(
            weighted,
            stat,
            lying,
            norm_mlp.reshape(-1, 128),
            w_out,
            jnp.swapaxes(w_gate, 0, 1),
            jnp.swapaxes(w_up, 0, 1),
            w_down,
            zs,
            seq,
        )
        output = jnp.swapaxes(
            output.reshape(steps, requests, pieces // 128, blocks, 128), 2, 3
        )
        return (output.reshape(hidden_in.shape), key_cache, value_cache)
    def by_head(value):
        value = jnp.moveaxis(value.reshape((KV, requests, steps, group) + value.shape[2:]), 1, 3)
        value = jnp.swapaxes(value, 1, 2)
        return value.reshape(seq, -1)

    def by_line(value):
        return by_head(value[:, :, :lines].reshape(KV, requests * lines))

    packed = jnp.concatenate(
        [
            by_head(weighted.astype(jnp.float32)),
            by_line(stat[:, :requests]),
            by_line(stat[:, requests:]),
        ],
        axis=1,
    )
    packed = lax.all_to_all(packed, "seq", split_axis=0, concat_axis=0, tiled=True)
    count = (H // seq) * rows
    part_acc = packed[:, : count * HD].reshape(seq, count, HD)
    part_top = packed[:, count * HD : count * (HD + 1)]
    part_sum = packed[:, count * (HD + 1) :]
    best = jnp.max(part_top, axis=0)
    share = jnp.exp(part_top - best[None])
    denominator = jnp.sum(share * part_sum, axis=0)
    numerator = jnp.sum(share[..., None] * part_acc, axis=0)
    heads = (numerator / denominator[:, None]).astype(jnp.bfloat16)
    heads = jnp.swapaxes(heads.reshape(H // seq, rows, HD), 0, 1).reshape(rows, -1)
    attended = lax.all_gather(heads, "seq", axis=1, tiled=True)
    branch_out = jnp.dot(
        attended, w_out.reshape(H * HD, blocks * pieces), preferred_element_type=jnp.float32
    ).reshape(rows, blocks, pieces)
    current = hidden_in.reshape(rows, blocks, pieces).astype(jnp.float32)
    middle = (current + branch_out).astype(jnp.bfloat16)
    rows_mid = lax.all_gather(middle, "seq", axis=2, tiled=True).astype(jnp.float32)
    inverse = lax.rsqrt(jnp.mean(rows_mid * rows_mid, axis=(1, 2), keepdims=True) + EPSILON)
    normed_mid = (rows_mid * inverse * norm_mlp.reshape(blocks, quarter)).astype(jnp.bfloat16)
    mine = lax.all_to_all(normed_mid, "req", split_axis=1, concat_axis=0, tiled=True).reshape(
        -1, quarter
    )
    gate_part = jnp.dot(mine, w_gate, preferred_element_type=jnp.float32).astype(jnp.bfloat16)
    up_part = jnp.dot(mine, w_up, preferred_element_type=jnp.float32).astype(jnp.bfloat16)
    gate_sum = lax.psum_scatter(gate_part, "req", scatter_dimension=0, tiled=True)
    up_sum = lax.psum_scatter(up_part, "req", scatter_dimension=0, tiled=True)
    hidden_part = (
        jax.nn.silu(gate_sum.astype(jnp.float32)) * up_sum.astype(jnp.float32)
    ).astype(jnp.bfloat16)
    hidden = lax.all_gather(hidden_part, "req", axis=0, tiled=True)
    down = jnp.dot(hidden, w_down, preferred_element_type=jnp.float32)
    sums = lax.psum_scatter(
        down.reshape(down.shape[0], 1, quarter).astype(jnp.bfloat16),
        "seq",
        scatter_dimension=2,
        tiled=True,
    ).astype(jnp.float32)
    back = lax.all_to_all(sums, "req", split_axis=0, concat_axis=1, tiled=True)
    output = (middle.astype(jnp.float32) + back).astype(jnp.bfloat16)
    return (output.reshape(hidden_in.shape), key_cache, value_cache)


def solution(mesh):
    in_specs = (
        P(None, "req", None, "seq"),
        P("req"),
        P("req", None),
        P(("req", "seq"), None, None),
        P(("req", "seq"), None, None),
        P(),
        P(None, "seq"),
        P("seq"),
        P(None, None, "seq"),
        P(),
        P("req", "seq"),
        P("req", "seq"),
        P("seq", "req"),
    )
    out_specs = (
        P(None, "req", None, "seq"),
        P(("req", "seq"), None, None),
        P(("req", "seq"), None, None),
    )
    return jax.shard_map(
        on_device, mesh=mesh, in_specs=in_specs, out_specs=out_specs, check_vma=False
    )
```

```python
import functools
import math

import jax
import jax.numpy as jnp
from jax import lax
from jax.experimental import pallas as pl
from jax.experimental.pallas import tpu as pltpu
from jax.sharding import PartitionSpec as P

D = 8192
H = 64
KV = 8
HD = 128
STEPS = 4


EPSILON = 1e-06
THETA = 1000000.0
NEGATIVE = -1e30


def rotate(heads, position):
    half = heads.shape[-1] // 2
    freq = THETA ** (-(jnp.arange(half, dtype=jnp.float32) * 2.0 / heads.shape[-1]))
    angle = position.astype(jnp.float32)[:, None, None] * freq[None, None, :]
    cosine = jnp.cos(angle)
    sine = jnp.sin(angle)
    first = heads[..., :half]
    second = heads[..., half:]
    return jnp.concatenate(
        [first * cosine - second * sine, second * cosine + first * sine], axis=-1
    )


MESH = pl.DeviceIdType.MESH


def greet(partners):
    barrier = pltpu.get_barrier_semaphore()
    for partner in partners:
        pl.semaphore_signal(barrier, inc=1, device_id=partner, device_id_type=MESH)
    pl.semaphore_wait(barrier, len(partners))


def remote(src, dst, send, recv, partner):
    return pltpu.make_async_remote_copy(
        src_ref=src,
        dst_ref=dst,
        send_sem=send,
        recv_sem=recv,
        device_id=partner,
        device_id_type=MESH,
    )


class Gather:
    def __init__(self, z, s, ss, dst, send, recv):
        def flip(value, bit):
            return value + bit - 2 * bit * lax.rem(lax.div(value, bit), 2)

        self.twin = flip(s, 1)
        self.peers = []
        for mask in range(1, ss // 2):
            value, bit = s, 2
            while bit < ss:
                if mask & (bit // 2):
                    value = flip(value, bit)
                bit *= 2
            self.peers.append(value)
        count = len(self.peers)
        self.slots = (
            [s, self.twin] + self.peers + [flip(peer, 1) for peer in self.peers]
        )
        twin = {"req": z, "seq": self.twin}
        self.partners = [twin] + [{"req": z, "seq": peer} for peer in self.peers]
        self.parts = list(zip(dst, send, recv))
        self.direct, self.onward = [], []
        for i, partner in enumerate(self.partners):
            self.direct.append(
                [remote(d.at[s], d.at[s], a.at[i], b.at[i], partner) for d, a, b in self.parts]
            )
        for i, peer in enumerate(self.peers):
            at = count + 1 + i
            self.onward.append(
                [remote(d.at[peer], d.at[peer], a.at[at], b.at[at], twin) for d, a, b in self.parts]
            )

    def start(self):
        for copies in self.direct:
            for copy in copies:
                copy.start()

    def wait(self, step):
        if step == 0:
            return
        if step <= len(self.direct):
            for copy in self.direct[step - 1]:
                copy.wait_recv()
            if step > 1:
                for copy in self.onward[step - 2]:
                    copy.start()
        else:
            for copy in self.onward[step - 1 - len(self.direct)]:
                copy.wait_recv()

    def wait_all(self):
        for step in range(len(self.slots)):
            self.wait(step)

    def wait_sent(self):
        for copies in self.direct + self.onward:
            for copy in copies:
                copy.wait_send()


WIDTH = 128
PANEL = 256
LAGS = (0, 10, 14, 33, 38, 46, 56)
RING = 6
KEPT = 4
EARLY = 5
NEXT = 10


def tail_kernel(
    zs,
    ss,
    width,
    acc_ref,
    stat_ref,
    x_ref,
    norm_hbm,
    wo_hbm,
    wg_hbm,
    wu_hbm,
    wd_hbm,
    out_ref,
    wo,
    wg,
    wu,
    wd,
    got_acc,
    got_stat,
    mixed,
    everyone,
    pick,
    masks,
    lay,
    mid,
    cut,
    square,
    gains,
    got,
    got_sq,
    normed,
    own_g,
    own_u,
    send_r,
    recv_r,
    send_l,
    recv_l,
    hid,
    down,
    parts,
    landed,
    sums,
    back,
    wo_sem,
    w_sem,
    wd_sem,
    in_sem,
    m_send,
    m_recv,
    h_send,
    h_recv,
    a_send,
    a_recv,
    b_send,
    b_recv,
    rs_send,
    rs_recv,
    ag_send,
    ag_recv,
    d_send,
    d_recv,
    e_send,
    e_recv,
):
    z = lax.axis_index("req")
    s = lax.axis_index("seq")
    f32, bf16 = jnp.float32, jnp.bfloat16
    rows, features = mid.shape
    pieces = features // zs
    stride = x_ref.shape[0] // rows
    per = H // ss
    units = wg.shape[0]
    half = zs * rows // 2
    starts = list(range(0, units, width))
    count = len(starts)
    sizes = [min(width, units - start) for start in starts]
    padded = [-(-size // 128) * 128 for size in sizes]
    ratio = PANEL // width
    tops = list(range(0, units, PANEL))
    panels = len(tops)
    heights = [min(PANEL, units - top) for top in tops]
    z_partners = [{"req": lax.rem(z + k, zs), "seq": s} for k in range(1, zs)]
    s_partners = [{"req": z, "seq": lax.rem(s + k, ss)} for k in range(1, ss)]
    attended = Gather(z, s, ss, [everyone], [h_send], [h_recv])
    depth = D // ss

    def wo_load(n):
        first_row = pl.multiple_of(attended.slots[n] * depth, depth)
        return pltpu.make_async_copy(
            wo_hbm.at[pl.ds(first_row, depth)], wo.at[n % KEPT], wo_sem.at[n % KEPT]
        )

    def wd_load(m):
        return pltpu.make_async_copy(
            wd_hbm.at[pl.ds(tops[m], heights[m])],
            wd.at[m % RING, pl.ds(0, heights[m])],
            wd_sem.at[m % RING],
        )

    def panel_loads(m):
        lines = pl.ds(tops[m], heights[m])
        return (
            pltpu.make_async_copy(wg_hbm.at[lines], wg.at[lines], w_sem.at[0, m]),
            pltpu.make_async_copy(wu_hbm.at[lines], wu.at[lines], w_sem.at[1, m]),
        )

    def start_panels(low, high):
        for m in range(min(low, panels), min(high, panels)):
            for load in panel_loads(m):
                load.start()

    staged = [
        pltpu.make_async_copy(acc_ref.at[s], got_acc.at[s], in_sem.at[0]),
        pltpu.make_async_copy(stat_ref.at[s], got_stat.at[s], in_sem.at[1]),
        pltpu.make_async_copy(norm_hbm, gains, in_sem.at[2]),
    ]
    for load in staged:
        load.start()
    for n in range(KEPT):
        wo_load(n).start()
    start_panels(0, EARLY)
    greet(z_partners + s_partners)

    first = []
    for k in range(1, ss):
        to = lax.rem(s + k, ss)
        first.append(
            remote(stat_ref.at[to], got_stat.at[s], m_send.at[1, k], m_recv.at[1, k], s_partners[k - 1])
        )
        first.append(
            remote(acc_ref.at[to], got_acc.at[s], m_send.at[0, k], m_recv.at[0, k], s_partners[k - 1])
        )
    for copy in first:
        copy.start()
    lay[...] = x_ref[...].astype(f32)
    span = zs * 256
    pick[...] = jnp.where(
        lax.div(lax.broadcasted_iota(jnp.int32, (256, span), 1), zs)
        == lax.broadcasted_iota(jnp.int32, (256, span), 0),
        1.0,
        0.0,
    ).astype(bf16)
    masks[...] = jnp.where(
        lax.rem(lax.broadcasted_iota(jnp.int32, masks.shape, 1), zs)
        == lax.div(lax.broadcasted_iota(jnp.int32, masks.shape, 0), rows),
        1.0,
        0.0,
    ).astype(bf16)
    for load in staged:
        load.wait()
    for copy in first:
        copy.wait_recv()
    start_panels(EARLY, NEXT)
    requests = stat_ref.shape[1] // 2
    lines = rows // requests * per
    best = got_stat[0, :requests]
    for other in range(1, ss):
        best = jnp.maximum(best, got_stat[other, :requests])
    shares = [jnp.exp(got_stat[other, :requests] - best) for other in range(ss)]
    denominator = shares[0] * got_stat[0, requests:]
    for other in range(1, ss):
        denominator = denominator + shares[other] * got_stat[other, requests:]
    lane = lax.broadcasted_iota(jnp.int32, denominator.shape, 1)
    denominator = jnp.where(lane < lines, denominator, 1.0)
    tall = jnp.transpose(jnp.concatenate([share / denominator for share in shares], axis=0))
    for request in range(requests):
        place = slice(request * lines, (request + 1) * lines)
        value = got_acc[0, place, :].astype(f32) * tall[:lines, request : request + 1]
        for other in range(1, ss):
            at = other * requests + request
            value = value + got_acc[other, place, :].astype(f32) * tall[:lines, at : at + 1]
        mixed[place, :] = value
    for head in range(per):
        column = [
            mixed[pl.ds(step * per + head, requests, stride=lines), :]
            for step in range(rows // requests)
        ]
        everyone[s, :, head * HD : (head + 1) * HD] = jnp.concatenate(column, axis=0).astype(bf16)
    attended.start()

    result = jnp.zeros((zs * rows, pieces), f32)
    for n in range(ss):
        attended.wait(n)
        block = everyone[attended.slots[n]]
        chunks = depth // 256
        tower = jnp.concatenate([block[:, c * 256 : (c + 1) * 256] for c in range(chunks)], axis=0)
        spread = jnp.dot(tower, pick[...], preferred_element_type=f32).astype(bf16)
        wo_load(n).wait()
        for c in range(chunks):
            line = spread[c * rows : (c + 1) * rows]
            left = jnp.concatenate([line] * zs, axis=0) * masks[...]
            right = wo[n % KEPT, c * 256 : (c + 1) * 256].reshape(span, pieces)
            result = result + jnp.dot(left, right, preferred_element_type=f32)
        if n + KEPT < ss:
            wo_load(n + KEPT).start()
    start_panels(NEXT, panels)
    for m in range(min(RING, panels)):
        wd_load(m).start()
    total = jnp.zeros((8, rows), f32)
    for block in range(zs):
        cols = slice(block * pieces, (block + 1) * pieces)
        came_in = jnp.concatenate(
            [
                lay[pl.ds(part * zs + block, rows, stride=stride), :]
                for part in range(pieces // 128)
            ],
            axis=1,
        )
        piece = (came_in + result[block * rows : (block + 1) * rows]).astype(bf16)
        mid[:, cols] = piece
        cut[block] = piece
        value = piece.astype(f32)
        total += lax.dot_general(
            jnp.ones((8, pieces), f32),
            value * value,
            (((1,), (1,)), ((), ())),
            precision=lax.Precision.HIGHEST,
            preferred_element_type=f32,
        )
    square[...] = jnp.zeros_like(square)
    square[:, :rows] = total
    second = []
    for k in range(1, zs):
        to = lax.rem(z + k, zs)
        second.append(
            remote(cut.at[to], got.at[s, z], a_send.at[0, k], a_recv.at[0, k], z_partners[k - 1])
        )
        second.append(
            remote(square, got_sq.at[s, z], a_send.at[1, k], a_recv.at[1, k], z_partners[k - 1])
        )
    for copy in second:
        copy.start()
    got[s, z] = cut[z]
    got_sq[s, z] = square[...]
    for copy in second:
        copy.wait_recv()
    blocks = Gather(z, s, ss, [got, got_sq], [b_send.at[0], b_send.at[1]], [b_recv.at[0], b_recv.at[1]])
    blocks.start()
    if sizes[-1] != padded[-1]:
        send_r[count - 1] = jnp.zeros_like(send_r[count - 1])
        send_l[count - 1] = jnp.zeros_like(send_l[count - 1])
        hid[panels - 1] = jnp.zeros_like(hid[panels - 1])
    down[...] = jnp.zeros_like(down)
    blocks.wait_all()
    for group in range(zs):
        line = got_sq[0, group]
        for other in range(1, ss):
            line = line + got_sq[other, group]
        spread = lax.dot_general(
            line[:, :rows],
            jnp.full((8, 128), 0.125, f32),
            (((0,), (0,)), ((), ())),
            precision=lax.Precision.HIGHEST,
            preferred_element_type=f32,
        )
        inverse = lax.rsqrt(spread / D + EPSILON)
        for other in range(ss):
            for part in range(pieces // 128):
                at = other * pieces + part * 128
                gain = gains[pl.ds(z * (ss * pieces // 128) + at // 128, 1), :]
                value = got[other, group, :, part * 128 : (part + 1) * 128].astype(f32)
                normed[group * rows : (group + 1) * rows, at : at + 128] = (
                    value * inverse * gain
                ).astype(bf16)

    right = {"req": lax.rem(z + 1, zs), "seq": s}
    left = {"req": lax.rem(z + zs - 1, zs), "seq": s}

    def reduce_copy(way, p):
        src, dst, to = ((send_r, recv_r, right), (send_l, recv_l, left))[way]
        lanes = pl.ds(0, 2 * padded[p])
        return remote(
            src.at[p, :, lanes], dst.at[p, :, lanes], rs_send.at[way, p], rs_recv.at[way, p], to
        )

    def hidden_copy(way, p):
        place = (
            p // ratio,
            pl.ds(half * (1 - way), half),
            pl.ds(p % ratio * width, padded[p]),
        )
        return remote(
            hid.at[place],
            hid.at[place],
            ag_send.at[way, p],
            ag_recv.at[way, p],
            (left, right)[way],
        )

    def reduce_step(way, p, place):
        size, pad = sizes[p], padded[p]
        base = half * (1 - way)
        cols = slice(starts[p], starts[p] + size)
        gate = own_g[base : base + half, cols]
        up = own_u[base : base + half, cols]
        if place > 0:
            reduce_copy(way, p).wait_recv()
            came = (recv_r, recv_l)[way]
            gate = gate + came[p, :, :size].astype(f32)
            up = up + came[p, :, pad : pad + size].astype(f32)
        if place < zs - 1:
            goes = (send_r, send_l)[way]
            goes[p, :, :size] = gate.astype(bf16)
            goes[p, :, pad : pad + size] = up.astype(bf16)
            reduce_copy(way, p).start()
        else:
            gate = gate.astype(bf16).astype(f32)
            up = up.astype(bf16).astype(f32)
            low = p % ratio * width
            hid[p // ratio, base : base + half, low : low + size] = (
                gate / (1.0 + jnp.exp(-gate)) * up
            ).astype(bf16)
            hidden_copy(way, p).start()

    def down_step(m):
        wd_load(m).wait()
        down[...] += jnp.dot(
            hid[m, :, : heights[m]], wd[m % RING, : heights[m], :], preferred_element_type=f32
        )
        if m + RING < panels:
            wd_load(m + RING).start()

    nt = (((1,), (1,)), ((), ()))
    lag = LAGS if zs == 4 else tuple(2 * i for i in range(2 * zs - 1))
    last = lag[2 * zs - 2]
    for i in range(count + last):
        if i < count and i % ratio == 0:
            m = i // ratio
            cols = slice(tops[m], tops[m] + heights[m])
            for load in panel_loads(m):
                load.wait()
            own_g[:, cols] = lax.dot_general(normed[...], wg[cols, :], nt, preferred_element_type=f32)
            own_u[:, cols] = lax.dot_general(normed[...], wu[cols, :], nt, preferred_element_type=f32)
        for zz in range(zs):

            @pl.when(z == zz)
            def _(zz=zz, i=i):
                order = (0, 1) if zz < zs // 2 else (1, 0)
                for way in order:
                    place = zz if way == 0 else zs - 1 - zz
                    p = i - lag[place]
                    if 0 <= p < count:
                        reduce_step(way, p, place)
                for way in order[::-1]:
                    place = zs - 1 - zz if way == 0 else zz
                    p = i - lag[zs - 1 + place]
                    if place > 0 and 0 <= p < count:
                        hidden_copy(way, p).wait_recv()
                        if place < zs - 1:
                            hidden_copy(way, p).start()

        p = i - last
        if p >= 0 and (p % ratio == ratio - 1 or p == count - 1):
            down_step(p // ratio)

    core, chip, chips = lax.rem(s, 2), lax.div(s, 2), ss // 2
    twin = {"req": z, "seq": attended.twin}

    def share(owner):
        return down[:, pl.ds(pl.multiple_of(owner * pieces, pieces), pieces)]

    targets = [lax.div(peer, 2) for peer in attended.peers] + [chip]
    third = []
    for n, target in enumerate(targets):
        parts[n] = share(target * 2 + 1 - core).astype(bf16)
        third.append(remote(parts.at[n], landed.at[n], d_send.at[n], d_recv.at[n], twin))
        third[-1].start()
    for n, target in enumerate(targets):
        third[n].wait_recv()
        both = (share(target * 2 + core) + landed[n].astype(f32)).astype(bf16)
        if n < chips - 1:
            parts[chips + n] = both
            third.append(
                remote(
                    parts.at[chips + n],
                    landed.at[chips + n],
                    d_send.at[chips + n],
                    d_recv.at[chips + n],
                    {"req": z, "seq": attended.peers[n]},
                )
            )
            third[-1].start()
    whole = both.astype(f32)
    for n in range(chips - 1):
        third[chips + n].wait_recv()
        whole = whole + landed[chips + n].astype(f32)
    for group in range(zs):
        sums[group] = whole[group * rows : (group + 1) * rows].astype(bf16)
    fourth = []
    for k in range(1, zs):
        to = lax.rem(z + k, zs)
        fourth.append(
            remote(sums.at[to], back.at[z], e_send.at[k], e_recv.at[k], z_partners[k - 1])
        )
    for copy in fourth:
        copy.start()
    back[z] = sums[z]
    for copy in fourth:
        copy.wait_recv()
    for block in range(zs):
        cols = slice(block * pieces, (block + 1) * pieces)
        value = mid[:, cols].astype(f32) + back[block].astype(f32)
        for part in range(pieces // 128):
            lay[pl.ds(part * zs + block, rows, stride=stride), :] = value[
                :, part * 128 : (part + 1) * 128
            ]
    out_ref[...] = lay[...].astype(bf16)

    for copy in first + second + third + fourth:
        copy.wait_send()
    attended.wait_sent()
    blocks.wait_sent()
    for way in range(2):
        for p in range(count):

            @pl.when(z != (zs - 1 if way == 0 else 0))
            def _(way=way, p=p):
                reduce_copy(way, p).wait_send()

            @pl.when(z != (0 if way == 0 else zs - 1))
            def _(way=way, p=p):
                hidden_copy(way, p).wait_send()


def tail(acc, stat, x, norm, w_out, w_gate, w_up, w_down, zs, ss):
    features = w_out.shape[1] * w_out.shape[2]
    rows = x.shape[0] * 128 // features
    pieces = features // zs
    units, depth = w_gate.shape
    quarter = w_down.shape[1]
    width = WIDTH
    count = -(-units // width)
    panels = -(-units // PANEL)
    everyone = zs * rows
    half = everyone // 2
    bf16, f32 = jnp.bfloat16, jnp.float32
    vmem = pl.BlockSpec(memory_space=pltpu.VMEM)
    hbm = pl.BlockSpec(memory_space=pl.ANY)
    dma = pltpu.SemaphoreType.DMA
    return pl.pallas_call(
        functools.partial(tail_kernel, zs, ss, width),
        name="tail",
        out_shape=jax.ShapeDtypeStruct(x.shape, bf16),
        in_specs=[hbm, hbm, vmem, hbm, hbm, hbm, hbm, hbm],
        out_specs=vmem,
        scratch_shapes=[
            pltpu.VMEM((KEPT, D // ss) + w_out.shape[1:], bf16),
            pltpu.VMEM(w_gate.shape, bf16),
            pltpu.VMEM(w_up.shape, bf16),
            pltpu.VMEM((RING, PANEL, quarter), bf16),
            pltpu.VMEM(acc.shape, bf16),
            pltpu.VMEM(stat.shape, f32),
            pltpu.VMEM(acc.shape[1:], f32),
            pltpu.VMEM((ss, rows, H // ss * HD), bf16),
            pltpu.VMEM((256, zs * 256), bf16),
            pltpu.VMEM((everyone, zs * 256), bf16),
            pltpu.VMEM(x.shape, f32),
            pltpu.VMEM((rows, features), bf16),
            pltpu.VMEM((zs, rows, pieces), bf16),
            pltpu.VMEM((8, 128), f32),
            pltpu.VMEM(norm.shape, f32),
            pltpu.VMEM((ss, zs, rows, pieces), bf16),
            pltpu.VMEM((ss, zs, 8, 128), f32),
            pltpu.VMEM((everyone, depth), bf16),
            pltpu.VMEM((everyone, units), f32),
            pltpu.VMEM((everyone, units), f32),
            pltpu.VMEM((count, half, 2 * width), bf16),
            pltpu.VMEM((count, half, 2 * width), bf16),
            pltpu.VMEM((count, half, 2 * width), bf16),
            pltpu.VMEM((count, half, 2 * width), bf16),
            pltpu.VMEM((panels, everyone, PANEL), bf16),
            pltpu.VMEM((everyone, quarter), f32),
            pltpu.VMEM((ss, everyone, pieces), bf16),
            pltpu.VMEM((ss, everyone, pieces), bf16),
            pltpu.VMEM((zs, rows, pieces), bf16),
            pltpu.VMEM((zs, rows, pieces), bf16),
            dma((KEPT,)),
            dma((2, panels)),
            dma((RING,)),
            dma((3,)),
            dma((2, ss)),
            dma((2, ss)),
            dma((ss,)),
            dma((ss,)),
            dma((2, zs)),
            dma((2, zs)),
            dma((2, ss)),
            dma((2, ss)),
            dma((2, count)),
            dma((2, count)),
            dma((2, count)),
            dma((2, count)),
            dma((ss,)),
            dma((ss,)),
            dma((zs,)),
            dma((zs,)),
        ],
        compiler_params=pltpu.CompilerParams(
            collective_id=0, has_side_effects=True, vmem_limit_bytes=61 * 2**20
        ),
    )(acc, stat, x, norm, w_out, w_gate, w_up, w_down)


def project_kernel(
    zs,
    ss,
    steps,
    x_ref,
    fixed_ref,
    w_hbm,
    q_ref,
    new_ref,
    w,
    lay,
    got,
    normed,
    columns_a,
    columns_b,
    spread,
    w_sem,
    a_send,
    a_recv,
    b_send,
    b_recv,
):
    z = lax.axis_index("req")
    s = lax.axis_index("seq")
    f32 = jnp.float32
    rows, features = got.shape[1:]
    requests = rows // steps
    blocks = zs
    pieces = features // blocks
    stride = x_ref.shape[0] // rows
    mine = w.shape[1]
    local = mine // HD
    group = H // KV
    parts = 4
    depth = D // parts
    cuts = [0, columns_a.shape[2], mine]
    halves = (columns_a, columns_b)

    def load(which, part):
        place = (pl.ds(part * depth, depth), pl.ds(cuts[which], cuts[which + 1] - cuts[which]))
        return pltpu.make_async_copy(w_hbm.at[place], w.at[place], w_sem.at[which, part])

    inputs = Gather(z, s, ss, [got], [a_send], [a_recv])
    outputs = [
        Gather(z, s, ss, [halves[i]], [b_send.at[i]], [b_recv.at[i]]) for i in range(2)
    ]
    for which in range(2):
        for part in range(parts):
            load(which, part).start()
    lay[...] = x_ref[...].astype(f32)
    for block in range(blocks):
        for part in range(pieces // 128):
            at = block * pieces + part * 128
            got[s, :, at : at + 128] = lay[
                pl.ds(part * blocks + block, rows, stride=stride), :
            ].astype(jnp.bfloat16)
    greet(inputs.partners)
    inputs.start()
    row = lax.broadcasted_iota(jnp.int32, (rows, HD), 0)
    lane = lax.broadcasted_iota(jnp.int32, (rows, HD), 1)
    lens = fixed_ref[(D + mine) // 128 : (D + mine) // 128 + 1, :]
    position = lax.div(row, requests).astype(f32) + jnp.sum(
        jnp.where(lane == lax.rem(row, requests), lens, 0.0), axis=1, keepdims=True
    )
    entry = lax.rem(lane, HD // 2).astype(f32)
    angle = position * jnp.exp(entry * (-2.0 * math.log(THETA) / HD))
    cosine = jnp.cos(angle)
    sine = jnp.where(lane < HD // 2, -jnp.sin(angle), jnp.sin(angle))
    inputs.wait_all()
    total = jnp.zeros((rows, 1), f32)
    for other in range(ss):
        value = got[other].astype(f32)
        total += jnp.sum(value * value, axis=1, keepdims=True)
    inverse = lax.rsqrt(total / D + EPSILON)
    for other in range(ss):
        for block in range(blocks):
            base = block * ss * pieces + other * pieces
            for line in range(pieces // 128):
                at = base + line * 128
                value = got[
                    other, :, block * pieces + line * 128 : block * pieces + (line + 1) * 128
                ].astype(f32)
                gain = fixed_ref[at // 128 : at // 128 + 1, :]
                normed[:, at : at + 128] = (value * inverse * gain).astype(jnp.bfloat16)
    bias = fixed_ref[D // 128 : (D + mine) // 128, :]
    for which in range(2):
        low, high = cuts[which], cuts[which + 1]
        result = jnp.zeros((rows, high - low), f32)
        for part in range(parts):
            load(which, part).wait()
            span = slice(part * depth, (part + 1) * depth)
            result += jnp.dot(normed[:, span], w[span, low:high], preferred_element_type=f32)
        for head in range(low // HD, high // HD):
            at = head * HD - low
            tile = (result[:, at : at + HD] + bias[head : head + 1]).astype(jnp.bfloat16).astype(f32)
            turned = tile * cosine + pltpu.roll(tile, HD // 2, axis=1) * sine
            halves[which][s, :, at : at + HD] = jnp.where(
                s * local + head < H + KV, turned, tile
            ).astype(jnp.bfloat16)
        outputs[which].start()
    for which in range(2):
        low, high = cuts[which], cuts[which + 1]
        outputs[which].wait_all()
        for head in range(H + 2 * KV):
            other, at = head // local, (head % local) * HD
            if not low <= at < high:
                continue
            tile = halves[which][other, :, at - low : at - low + HD].astype(f32)
            if head < H:
                for step in range(steps):
                    base = (head // group) * steps * group + step * group + head % group
                    spread[pl.ds(base, requests, stride=H * steps), :] = tile[
                        step * requests : (step + 1) * requests
                    ]
            else:
                at = ((head - H) % KV) * HD
                new_ref[(head - H) // KV, :, at : at + HD] = tile
    q_ref[...] = spread[...].astype(jnp.bfloat16)
    inputs.wait_sent()
    for output in outputs:
        output.wait_sent()


def project(lens, x, norm, bias, w, zs, ss, steps):
    features = D // ss
    rows = x.shape[0] * 128 // features
    mine = w.shape[1]
    fixed = jnp.concatenate(
        [
            norm,
            bias.astype(jnp.float32),
            lens.astype(jnp.float32),
            jnp.zeros(128 - lens.shape[0], jnp.float32),
        ]
    ).reshape(-1, 128)
    first = mine // HD * 3 // 5 * HD
    bf16, f32 = jnp.bfloat16, jnp.float32
    vmem = pl.BlockSpec(memory_space=pltpu.VMEM)
    dma = pltpu.SemaphoreType.DMA
    return pl.pallas_call(
        functools.partial(project_kernel, zs, ss, steps),
        name="project",
        out_shape=(
            jax.ShapeDtypeStruct((rows * H, HD), bf16),
            jax.ShapeDtypeStruct((2, rows, KV * HD), f32),
        ),
        in_specs=[
            vmem,
            vmem,
            pl.BlockSpec(memory_space=pl.ANY),
        ],
        out_specs=(vmem, vmem),
        scratch_shapes=[
            pltpu.VMEM(w.shape, bf16),
            pltpu.VMEM(x.shape, f32),
            pltpu.VMEM((ss, rows, features), bf16),
            pltpu.VMEM((rows, D), bf16),
            pltpu.VMEM((ss, rows, first), bf16),
            pltpu.VMEM((ss, rows, mine - first), bf16),
            pltpu.VMEM((rows * H, HD), f32),
            dma((2, 4)),
            dma((ss,)),
            dma((ss,)),
            dma((2, ss)),
            dma((2, ss)),
        ],
        compiler_params=pltpu.CompilerParams(
            collective_id=1, has_side_effects=True, vmem_limit_bytes=48 * 2**20
        ),
    )(x, fixed, w)


def attend_kernel(
    steps,
    table_ref,
    lens_ref,
    q_ref,
    new_ref,
    k_hbm,
    v_hbm,
    acc_ref,
    stat_ref,
    ko_hbm,
    vo_hbm,
    keys,
    values,
    wide,
    scores,
    probs,
    acc,
    in_sem,
    out_sem,
):
    f32, bf16 = jnp.float32, jnp.bfloat16
    slots, page, _ = keys.shape
    requests, most = table_ref.shape
    group = H // KV
    lines = steps * group
    block = KV * lines
    loads = [
        (
            pltpu.make_async_copy(k_hbm.at[j], keys.at[j], in_sem.at[0, j]),
            pltpu.make_async_copy(v_hbm.at[j], values.at[j], in_sem.at[1, j]),
        )
        for j in range(slots)
    ]
    for load in loads:
        load[0].start()
    for load in loads:
        load[1].start()
    stores = [
        (
            pltpu.make_async_copy(keys.at[j], ko_hbm.at[j], out_sem.at[0, j]),
            pltpu.make_async_copy(values.at[j], vo_hbm.at[j], out_sem.at[1, j]),
        )
        for j in range(slots)
    ]
    base = lax.axis_index("seq") * slots
    table = table_ref[...]
    code = (
        lax.broadcasted_iota(jnp.int32, table.shape, 0) * most
        + lax.broadcasted_iota(jnp.int32, table.shape, 1)
        + 1
    ).astype(f32)
    owners, starts, lives = [], [], []
    for j in range(slots):
        found = jnp.max(jnp.where(table == base + j, code, 0.0)).astype(jnp.int32)
        place = jnp.maximum(found - 1, 0)
        owner = lax.div(place, most)
        owners.append(owner)
        lives.append(found > 0)
        starts.append(lens_ref[owner] - (place - owner * most) * page)
    wide[...] = jnp.zeros_like(wide)
    acc[...] = jnp.zeros_like(acc)
    at_request = lax.broadcasted_iota(jnp.int32, (requests, block), 0)
    token = lax.broadcasted_iota(jnp.int32, (page, block), 0)
    step_of = lax.div(lax.rem(lax.broadcasted_iota(jnp.int32, (page, block), 1), lines), group)
    ahead = token - step_of
    row = lax.broadcasted_iota(jnp.int32, (page, 1), 0)
    scale = 1.0 / math.sqrt(HD)
    top = jnp.full((requests, block), NEGATIVE, f32)
    for j in range(slots):
        owner, start, live = owners[j], starts[j], lives[j]
        for which, buffer in ((0, keys), (1, values)):
            loads[j][which].wait()

            @pl.when(jnp.logical_and(live, jnp.logical_and(start > -steps, start < page)))
            def _(which=which, buffer=buffer, owner=owner, start=start, j=j):
                value = buffer[j].astype(f32)
                for step in range(steps):
                    fresh = new_ref[which, pl.ds(step * requests + owner, 1), :]
                    value = jnp.where(row == start + step, fresh, value)
                buffer[j] = value.astype(bf16)

            stores[j][which].start()
        query = q_ref[pl.ds(pl.multiple_of(owner * block, block), block), :]
        for k in range(KV):
            wide[j % 2, k * lines : (k + 1) * lines, k * HD : (k + 1) * HD] = query[
                k * lines : (k + 1) * lines
            ]
        score = (
            lax.dot_general(
                keys[j], wide[j % 2], (((1,), (1,)), ((), ())), preferred_element_type=f32
            )
            * scale
        )
        limit = jnp.where(live, start, -2 * page * most)
        score = jnp.where(ahead <= limit, score, NEGATIVE)
        scores[j] = score
        best = jnp.max(score, axis=0, keepdims=True)
        top = jnp.where(at_request == owner, jnp.maximum(top, best), top)
    total = jnp.zeros((requests, block), f32)
    for j in range(slots):
        owner = owners[j]
        best = jnp.max(jnp.where(at_request == owner, top, NEGATIVE), axis=0, keepdims=True)
        score = scores[j]
        prob = jnp.where(score > 0.5 * NEGATIVE, jnp.exp(score - best), 0.0)
        prob = prob.astype(bf16).astype(f32)
        part = jnp.sum(prob, axis=0, keepdims=True)
        total = jnp.where(at_request == owner, total + part, total)
        probs[j] = jnp.transpose(prob).astype(bf16)
    for j in range(slots):
        for k in range(KV):
            part = jnp.dot(
                probs[j, k * lines : (k + 1) * lines, :],
                values[j, :, k * HD : (k + 1) * HD],
                preferred_element_type=f32,
            )
            place = pl.ds(pl.multiple_of(owners[j] * lines, lines), lines)
            acc[k, place, :] += part
    acc_ref[...] = acc[...].astype(bf16)
    stat_ref[...] = jnp.zeros_like(stat_ref)
    for k in range(KV):
        stat_ref[k, :requests, :lines] = top[:, k * lines : (k + 1) * lines]
        stat_ref[k, requests:, :lines] = total[:, k * lines : (k + 1) * lines]
    for store in stores:
        store[0].wait()
        store[1].wait()


def attend(table, lens, q, new, key_cache, value_cache, steps):
    slots, page, width = key_cache.shape
    requests = table.shape[0]
    lines = steps * (H // KV)
    bf16, f32 = jnp.bfloat16, jnp.float32
    vmem = pl.BlockSpec(memory_space=pltpu.VMEM)
    hbm = pl.BlockSpec(memory_space=pl.ANY)
    dma = pltpu.SemaphoreType.DMA
    return pl.pallas_call(
        functools.partial(attend_kernel, steps),
        name="attend",
        out_shape=(
            jax.ShapeDtypeStruct((KV, requests * lines, HD), bf16),
            jax.ShapeDtypeStruct((KV, 2 * requests, 128), f32),
            jax.ShapeDtypeStruct(key_cache.shape, bf16),
            jax.ShapeDtypeStruct(value_cache.shape, bf16),
        ),
        in_specs=[vmem, pl.BlockSpec(memory_space=pltpu.SMEM), vmem, vmem, hbm, hbm],
        out_specs=(vmem, vmem, hbm, hbm),
        scratch_shapes=[
            pltpu.VMEM(key_cache.shape, bf16),
            pltpu.VMEM(value_cache.shape, bf16),
            pltpu.VMEM((2, KV * lines, width), bf16),
            pltpu.VMEM((slots, page, KV * lines), f32),
            pltpu.VMEM((slots, KV * lines, page), bf16),
            pltpu.VMEM((KV, requests * lines, HD), f32),
            dma((2, slots)),
            dma((2, slots)),
        ],
        compiler_params=pltpu.CompilerParams(vmem_limit_bytes=32 * 2**20),
    )(table, lens, q, new, key_cache, value_cache)


def on_device(
    hidden_in,
    cache_lens,
    page_table,
    key_cache,
    value_cache,
    norm_attn,
    w_qkv,
    b_qkv,
    w_out,
    norm_mlp,
    w_gate,
    w_up,
    w_down,
):
    steps, requests, blocks, pieces = hidden_in.shape
    rows = steps * requests
    group = H // KV
    quarter = D // blocks
    seq = quarter // pieces
    zs = D // w_gate.shape[0]
    fast = (
        pieces % 128 == 0
        and w_qkv.shape[1] % 128 == 0
        and zs == blocks
        and zs % 2 == 0
        and rows <= 128
        and rows % 16 == 0
        and requests == 8
        and seq == KV
        and pieces == 256
    )
    lines = steps * group
    if fast:
        lying = jnp.swapaxes(
            hidden_in.reshape(steps, requests, blocks, pieces // 128, 128), 2, 3
        ).reshape(-1, 128)
        queries, fresh = project(
            cache_lens,
            lying,
            norm_attn,
            b_qkv,
            w_qkv,
            zs,
            seq,
            steps,
        )
    else:
        flat = (
            lax.all_gather(hidden_in, "seq", axis=3, tiled=True).reshape(rows, D).astype(jnp.float32)
        )
        normed = (
            flat * lax.rsqrt(jnp.mean(flat * flat, axis=1, keepdims=True) + EPSILON) * norm_attn
        ).astype(jnp.bfloat16)
        columns = (
            jnp.dot(normed, w_qkv, preferred_element_type=jnp.float32) + b_qkv.astype(jnp.float32)
        ).astype(jnp.bfloat16)
        projected = lax.all_gather(columns, "seq", axis=1, tiled=True)
        position = (
            jnp.arange(steps, dtype=jnp.int32)[:, None] + cache_lens[None, :]
        ).reshape(rows)
        rotated = rotate(
            projected[:, : (H + KV) * HD].reshape(rows, H + KV, HD).astype(jnp.float32), position
        ).astype(jnp.bfloat16)
        queries = jnp.transpose(
            rotated[:, :H].reshape(steps, requests, KV, group, HD), (1, 2, 0, 3, 4)
        ).reshape(rows * H, HD)
        fresh = jnp.stack(
            [rotated[:, H:].reshape(rows, KV * HD), projected[:, (H + KV) * HD :]]
        ).astype(jnp.float32)
    weighted, stat, key_cache, value_cache = attend(
        page_table, cache_lens, queries, fresh, key_cache, value_cache, steps
    )

    if fast:
        output = tail(
            weighted,
            stat,
            lying,
            norm_mlp.reshape(-1, 128),
            w_out,
            jnp.swapaxes(w_gate, 0, 1),
            jnp.swapaxes(w_up, 0, 1),
            w_down,
            zs,
            seq,
        )
        output = jnp.swapaxes(
            output.reshape(steps, requests, pieces // 128, blocks, 128), 2, 3
        )
        return (output.reshape(hidden_in.shape), key_cache, value_cache)
    def by_head(value):
        value = jnp.moveaxis(value.reshape((KV, requests, steps, group) + value.shape[2:]), 1, 3)
        value = jnp.swapaxes(value, 1, 2)
        return value.reshape(seq, -1)

    def by_line(value):
        return by_head(value[:, :, :lines].reshape(KV, requests * lines))

    packed = jnp.concatenate(
        [
            by_head(weighted.astype(jnp.float32)),
            by_line(stat[:, :requests]),
            by_line(stat[:, requests:]),
        ],
        axis=1,
    )
    packed = lax.all_to_all(packed, "seq", split_axis=0, concat_axis=0, tiled=True)
    count = (H // seq) * rows
    part_acc = packed[:, : count * HD].reshape(seq, count, HD)
    part_top = packed[:, count * HD : count * (HD + 1)]
    part_sum = packed[:, count * (HD + 1) :]
    best = jnp.max(part_top, axis=0)
    share = jnp.exp(part_top - best[None])
    denominator = jnp.sum(share * part_sum, axis=0)
    numerator = jnp.sum(share[..., None] * part_acc, axis=0)
    heads = (numerator / denominator[:, None]).astype(jnp.bfloat16)
    heads = jnp.swapaxes(heads.reshape(H // seq, rows, HD), 0, 1).reshape(rows, -1)
    attended = lax.all_gather(heads, "seq", axis=1, tiled=True)
    branch_out = jnp.dot(
        attended, w_out.reshape(H * HD, blocks * pieces), preferred_element_type=jnp.float32
    ).reshape(rows, blocks, pieces)
    current = hidden_in.reshape(rows, blocks, pieces).astype(jnp.float32)
    middle = (current + branch_out).astype(jnp.bfloat16)
    rows_mid = lax.all_gather(middle, "seq", axis=2, tiled=True).astype(jnp.float32)
    inverse = lax.rsqrt(jnp.mean(rows_mid * rows_mid, axis=(1, 2), keepdims=True) + EPSILON)
    normed_mid = (rows_mid * inverse * norm_mlp.reshape(blocks, quarter)).astype(jnp.bfloat16)
    mine = lax.all_to_all(normed_mid, "req", split_axis=1, concat_axis=0, tiled=True).reshape(
        -1, quarter
    )
    gate_part = jnp.dot(mine, w_gate, preferred_element_type=jnp.float32).astype(jnp.bfloat16)
    up_part = jnp.dot(mine, w_up, preferred_element_type=jnp.float32).astype(jnp.bfloat16)
    gate_sum = lax.psum_scatter(gate_part, "req", scatter_dimension=0, tiled=True)
    up_sum = lax.psum_scatter(up_part, "req", scatter_dimension=0, tiled=True)
    hidden_part = (
        jax.nn.silu(gate_sum.astype(jnp.float32)) * up_sum.astype(jnp.float32)
    ).astype(jnp.bfloat16)
    hidden = lax.all_gather(hidden_part, "req", axis=0, tiled=True)
    down = jnp.dot(hidden, w_down, preferred_element_type=jnp.float32)
    sums = lax.psum_scatter(
        down.reshape(down.shape[0], 1, quarter).astype(jnp.bfloat16),
        "seq",
        scatter_dimension=2,
        tiled=True,
    ).astype(jnp.float32)
    back = lax.all_to_all(sums, "req", split_axis=0, concat_axis=1, tiled=True)
    output = (middle.astype(jnp.float32) + back).astype(jnp.bfloat16)
    return (output.reshape(hidden_in.shape), key_cache, value_cache)


def solution(mesh):
    in_specs = (
        P(None, "req", None, "seq"),
        P("req"),
        P("req", None),
        P(("req", "seq"), None, None),
        P(("req", "seq"), None, None),
        P(),
        P(None, "seq"),
        P("seq"),
        P(None, None, "seq"),
        P(),
        P("req", "seq"),
        P("req", "seq"),
        P("seq", "req"),
    )
    out_specs = (
        P(None, "req", None, "seq"),
        P(("req", "seq"), None, None),
        P(("req", "seq"), None, None),
    )
    return jax.shard_map(
        on_device, mesh=mesh, in_specs=in_specs, out_specs=out_specs, check_vma=False
    )
```
